32 devices in a mesh: seq: 2 (over x), batch: 4 (over y, core), head: 4 (over z).
Axes of the slice: x: 2, y: 2, z: 4, core: 2. Of those that a mesh axis runs over, the one named last changes fastest.
Arguments:
- hidden: bfloat16 [4, 256, 16384], P('batch', None, 'seq'), may hold values from -760 to 760
- gain: float32 [16384], P('seq'), may hold values from 0.5 to 1.5
- key_weight: bfloat16 [16384, 1024], P('seq', 'head'), may hold values from -0.046875 to 0.046875
- value_weight: bfloat16 [16384, 1024], P('seq', 'head'), may hold values from -0.046875 to 0.046875
- positions: int32 [4, 256], P('batch', 'seq'), may hold values from 0 to 32767
- initial_basis: float32 [2048, 256], P('head'), may hold values from -6 to 6
Outputs:
- basis: float32 [2048, 256], P('head')
The draws below stay inside these ranges and needn't reach their ends.
All inputs are finite; a program needn't handle non-finite values.
Results may differ from the reference program's by a relative error of at most 0.0063.
Values may be sent and summed in bfloat16 or wider, within the bound.
A program may use at most 64 MiB of HBM per device.

```python
import math
import jax
import jax.numpy as jnp
from jax import lax

D = 16384
KV_HEADS = 8
HEAD_DIM = 128
RANK = 256
ITERS = 4
SEQ_LEN = 256
SEQS = 4
JOINT = 2048


def draw_hidden(key, part):
    subkeys = jax.random.split(key, 4)
    full_shape = (SEQS, SEQ_LEN, D)
    group_width = D // 64
    block_scale = jnp.exp(jax.random.uniform(subkeys[1], (SEQS, SEQ_LEN, 64, 1), jnp.float32, math.log(0.3), math.log(3.0)))
    rising = jnp.exp(math.log(3.0) * jnp.arange(D, dtype=jnp.float32) / D) * jax.random.uniform(subkeys[2], (D,), jnp.float32, 0.7, 1.4)
    token_scale = jnp.exp(jax.random.uniform(subkeys[0], (SEQS, SEQ_LEN, 1), jnp.float32, 0.0, math.log(10.0)))
    base = jnp.clip(jax.random.normal(subkeys[3], full_shape, jnp.float32), -6.0, 6.0)
    values = (base.reshape(SEQS, SEQ_LEN, 64, group_width) * block_scale).reshape(full_shape)
    return (values * rising * token_scale).astype(jnp.bfloat16)


def with_ends(drawn, own_key, low, largest):
    dims = drawn.shape
    spot = [jax.random.randint(jax.random.fold_in(own_key, axis), (), 0, dims[axis]) for axis in range(len(dims))]
    drawn = drawn.at[tuple(spot)].set(low)
    longest = dims.index(max(dims))
    spot[longest] = (spot[longest] + 1) % dims[longest]
    return drawn.at[tuple(spot)].set(largest)


def steps_of(key, extent, cuts, low, high):
    level, own = 1.0, jax.random.fold_in(key, 6)
    for axis_at, shards_of in cuts:
        heights = jnp.exp(jax.random.uniform(jax.random.fold_in(own, axis_at), (shards_of,), jnp.float32, low / len(cuts), high / len(cuts)))
        level = level * jnp.repeat(heights, extent[axis_at] // shards_of).reshape([-1 if axis == axis_at else 1 for axis in range(len(extent))])
    return level


def scatter_about(key, dims, width, limit, pieces=(), held_as=jnp.bfloat16):
    loudness = steps_of(key, dims, pieces, -0.22, 0.18) if pieces else 1.0
    values = jax.random.normal(key, dims, jnp.float32) * width * loudness
    return jnp.minimum(jnp.maximum(values, -limit), limit).astype(held_as)


def setup_inputs(seed: int = 0) -> dict:
    seeds = jax.random.split(jax.random.key(seed), 7)
    hidden = draw_hidden(jax.random.fold_in(seeds[6], 71), 0)
    gain = jnp.clip(1.0 + 0.1 * jax.random.normal(seeds[1], (D,), jnp.float32), 0.5, 1.5)
    key_weight = scatter_about(seeds[2], (D, KV_HEADS * HEAD_DIM), D ** -0.5, 0.046875, ((0, 2), (1, 4)))
    value_weight = scatter_about(seeds[3], (D, KV_HEADS * HEAD_DIM), D ** -0.5, 0.046875, ((0, 2), (1, 4)))
    positions = with_ends(jax.random.randint(seeds[4], (SEQS, SEQ_LEN), 0, 32768), jax.random.fold_in(seeds[4], 1), 0, 32767).astype(jnp.int32)
    initial_basis = scatter_about(seeds[5], (JOINT, RANK), 1.0, 6.0, ((0, 4),), jnp.float32)
    return {"hidden": hidden, "gain": gain, "key_weight": key_weight, "value_weight": value_weight, "positions": positions, "initial_basis": initial_basis}


EPSILON = 1e-05
ROTARY_BASE = 500000.0

def rotary(head_rows, position_row):
    half_width = head_rows.shape[-1] // 2
    index_row = jnp.arange(half_width, dtype=jnp.float32)
    frequency = jnp.exp(index_row * (-math.log(ROTARY_BASE) / half_width))
    angles = position_row.astype(jnp.float32)[:, None] * frequency[None, :]
    cosine = jnp.cos(angles)[:, None, :]
    sine_part = jnp.sin(angles)[:, None, :]
    first_half = head_rows[..., :half_width]
    second_half = head_rows[..., half_width:]
    return jnp.concatenate([first_half * cosine - second_half * sine_part, second_half * cosine + first_half * sine_part], axis=-1)

def joint_of(hidden_rows, gain, key_weight, value_weight, position_row):
    widened = hidden_rows.astype(jnp.float32)
    squares = lax.optimization_barrier(jnp.sum(widened * widened, axis=1))
    inverse_scale = lax.rsqrt(squares / D + EPSILON)
    scaled = (widened * gain).astype(jnp.bfloat16)
    key_proj = jnp.dot(scaled.astype(jnp.float32), key_weight.astype(jnp.float32), preferred_element_type=jnp.float32) * inverse_scale[:, None]
    value_proj = jnp.dot(scaled.astype(jnp.float32), value_weight.astype(jnp.float32), preferred_element_type=jnp.float32) * inverse_scale[:, None]
    length = hidden_rows.shape[0]
    key_rows = rotary(key_proj.reshape(length, -1, HEAD_DIM), position_row)
    value_rows = value_proj.reshape(length, -1, HEAD_DIM)
    return jnp.stack([key_rows, value_rows], axis=2).reshape(length, -1).astype(jnp.bfloat16)

def reference(hidden, gain, key_weight, value_weight, positions, initial_basis):

    def add_sequence(total, items):
        hidden_rows, position_row = items
        joint_rows = joint_of(hidden_rows, gain, key_weight, value_weight, position_row)
        return (total + jnp.dot(joint_rows.T.astype(jnp.float32), joint_rows.astype(jnp.float32), preferred_element_type=jnp.float32), None)
    total, unused = lax.scan(add_sequence, jnp.zeros((JOINT, JOINT), jnp.float32), (hidden, positions))
    covariance = total / (SEQS * SEQ_LEN)
    basis = initial_basis
    for iteration in range(ITERS):
        images = jnp.dot(covariance.astype(jnp.float32), basis.astype(jnp.float32), precision=lax.Precision.HIGHEST, preferred_element_type=jnp.float32)
        gram_matrix = jnp.dot(images.T.astype(jnp.float32), images.astype(jnp.float32), precision=lax.Precision.HIGHEST, preferred_element_type=jnp.float32) / JOINT
        factor = jnp.linalg.cholesky(gram_matrix)
        basis = lax.linalg.triangular_solve(factor, images, left_side=False, lower=True, transpose_a=True)
    return basis
```

```python
import math

import jax
import jax.numpy as jnp
from jax import lax
from jax.experimental import pallas as pl
from jax.experimental.pallas import tpu as pltpu
from jax.sharding import PartitionSpec as P

D = 16384
HEAD_DIM = 128
ITERS = 4


EPSILON = 1e-05
ROTARY_BASE = 500000.0


def rotary(head_rows, position_row):
    half_width = head_rows.shape[-1] // 2
    index_row = jnp.arange(half_width, dtype=jnp.float32)
    frequency = jnp.exp(index_row * (-math.log(ROTARY_BASE) / half_width))
    angles = position_row.astype(jnp.float32)[:, None] * frequency[None, :]
    cosine = jnp.cos(angles)[:, None, :]
    sine_part = jnp.sin(angles)[:, None, :]
    first_half = head_rows[..., :half_width]
    second_half = head_rows[..., half_width:]
    return jnp.concatenate(
        [
            first_half * cosine - second_half * sine_part,
            second_half * cosine + first_half * sine_part,
        ],
        axis=-1,
    )


def whole_of(basis_block):
    return lax.all_gather(basis_block, "head", axis=0, tiled=True)


def total_squares(local_squares, local_tokens):
    all_squares = lax.psum(local_squares, "seq")
    return lax.dynamic_slice_in_dim(all_squares, lax.axis_index("seq") * local_tokens, local_tokens)


def gram_of(images):
    return lax.dot_general(
        images,
        images,
        (((0,), (0,)), ((), ())),
        precision=lax.Precision.HIGHEST,
        preferred_element_type=jnp.float32,
    )


def orthonormal(images, gram_matrix):
    factor = jnp.linalg.cholesky(gram_matrix)
    return lax.linalg.triangular_solve(
        factor, images, left_side=False, lower=True, transpose_a=True
    )


LANES = 128
SUBLANES = 8


def dot_of(left, right, left_axis, right_axis, precision=None):
    return lax.dot_general(
        left,
        right,
        (((left_axis,), (right_axis,)), ((), ())),
        precision=precision,
        preferred_element_type=jnp.float32,
    )


def exact(left, right, left_axis, right_axis):
    return dot_of(left, right, left_axis, right_axis, lax.Precision.HIGHEST)


def halves_of(value):
    high = value.astype(jnp.bfloat16)
    return high, (value - high.astype(jnp.float32)).astype(jnp.bfloat16)


def inverse_factor(matrix):
    size = matrix.shape[0]
    rows = lax.broadcasted_iota(jnp.int32, (SUBLANES, size), 0)
    lanes = lax.broadcasted_iota(jnp.int32, (SUBLANES, size), 1)
    groups = size // SUBLANES
    left = [matrix[SUBLANES * g : SUBLANES * (g + 1)] for g in range(groups)]
    right = [jnp.where(lanes == rows + SUBLANES * g, 1.0, 0.0) for g in range(groups)]
    done = []

    def spread_row(value, at):
        return jnp.broadcast_to(value[at : at + 1, :], (SUBLANES, size))

    def spread_lane(value, at):
        return jnp.broadcast_to(value[:, at : at + 1], (SUBLANES, size))

    for pivot in range(0, size, 2):
        own, at = pivot // SUBLANES, pivot % SUBLANES
        top, low = spread_row(left[own], at), spread_row(left[own], at + 1)
        top_right, low_right = spread_row(right[own], at), spread_row(right[own], at + 1)
        first, cross, last = (
            spread_lane(top, pivot),
            spread_lane(top, pivot + 1),
            spread_lane(low, pivot + 1),
        )
        scale = 1.0 / (first * last - cross * cross)
        mix_top = (top * last - low * cross) * scale
        mix_low = (low * first - top * cross) * scale
        mix_top_right = (top_right * last - low_right * cross) * scale
        mix_low_right = (low_right * first - top_right * cross) * scale
        ratio = cross / first
        done.append(
            (
                top_right * lax.rsqrt(first),
                (low_right - ratio * top_right) * lax.rsqrt(last - ratio * cross),
            )
        )
        for g in range(own, groups):
            if g == own and at + 2 >= SUBLANES:
                continue
            one, two = spread_lane(left[g], pivot), spread_lane(left[g], pivot + 1)
            if g == own:
                one = jnp.where(rows > at + 1, one, 0.0)
                two = jnp.where(rows > at + 1, two, 0.0)
            left[g] = left[g] - one * mix_top - two * mix_low
            right[g] = right[g] - one * mix_top_right - two * mix_low_right
    blocks = []
    for g in range(groups):
        block = jnp.zeros((SUBLANES, size), jnp.float32)
        for pair in range(SUBLANES // 2):
            upper, lower = done[g * SUBLANES // 2 + pair]
            block = jnp.where(rows == 2 * pair, upper, block)
            block = jnp.where(rows == 2 * pair + 1, lower, block)
        blocks.append(block)
    return jnp.concatenate(blocks, axis=0)


def iterate_kernel(joint_ref, basis_ref, own_ref, out_ref, high_ref, low_ref, rows_ref, images_ref, gram_ref, inverse_ref):
    tokens, joint = joint_ref.shape
    rank = basis_ref.shape[1]
    panels = rank // LANES
    strip = 256
    for start in range(0, tokens, strip):
        kernel_rows = dot_of(joint_ref[start : start + strip, :], joint_ref[...], 1, 1) * (1.0 / tokens)
        high, low = halves_of(kernel_rows)
        high_ref[start : start + strip, :] = high
        low_ref[start : start + strip, :] = low
    basis_high, basis_low = halves_of(basis_ref[...])
    rows_ref[...] = dot_of(joint_ref[...], basis_high, 1, 0) + dot_of(joint_ref[...], basis_low, 1, 0)

    def step(iteration, carry):
        rows_high, rows_low = halves_of(rows_ref[...])
        images_ref[...] = (
            dot_of(high_ref[...], rows_high, 1, 0)
            + dot_of(high_ref[...], rows_low, 1, 0)
            + dot_of(low_ref[...], rows_high, 1, 0)
        )
        gram_ref[...] = exact(rows_ref[...], images_ref[...], 0, 0) * (1.0 / (tokens * joint))

        @pl.when(iteration < ITERS - 1)
        def _():
            rows_ref[...] = images_ref[...]

        def panel_step(panel, inner):
            at = pl.ds(pl.multiple_of(panel * LANES, LANES), LANES)
            inverse = inverse_factor(gram_ref[at, at])
            scaled = exact(inverse, gram_ref[at, :], 1, 0)
            lane = lax.broadcasted_iota(jnp.int32, scaled.shape, 1)
            scaled = jnp.where(lane >= (panel + 1) * LANES, scaled, 0.0)
            gram_ref[...] -= exact(scaled, scaled, 0, 0)
            columns = exact(rows_ref[:, at], inverse, 1, 1)
            rows_ref[...] -= exact(columns, scaled, 1, 0)
            rows_ref[:, at] = columns
            return inner

        lax.fori_loop(0, panels, panel_step, 0)
        return carry

    lax.fori_loop(0, ITERS, step, 0)
    rows_high, rows_low = halves_of(rows_ref[...])
    out_ref[...] = (dot_of(own_ref[...], rows_high, 0, 0) + dot_of(own_ref[...], rows_low, 0, 0)) * (1.0 / tokens)


def iterate(joint_all, basis_all, own_rows):
    tokens, joint = joint_all.shape
    rank = basis_all.shape[1]
    return pl.pallas_call(
        iterate_kernel,
        out_shape=jax.ShapeDtypeStruct((own_rows.shape[1], rank), jnp.float32),
        in_specs=[pl.BlockSpec(memory_space=pltpu.VMEM)] * 3,
        out_specs=pl.BlockSpec(memory_space=pltpu.VMEM),
        scratch_shapes=[
            pltpu.VMEM((tokens, tokens), jnp.bfloat16),
            pltpu.VMEM((tokens, tokens), jnp.bfloat16),
            pltpu.VMEM((tokens, rank), jnp.float32),
            pltpu.VMEM((tokens, rank), jnp.float32),
            pltpu.VMEM((rank, rank), jnp.float32),
            pltpu.VMEM((LANES, LANES), jnp.float32),
        ],
        compiler_params=pltpu.CompilerParams(vmem_limit_bytes=60 * 2**20),
    )(joint_all, basis_all, own_rows)


def body(hidden, gain, key_weight, value_weight, positions, initial_basis):
    hidden_rows = hidden[0]
    local_tokens = positions.shape[1]
    widened = hidden_rows.astype(jnp.float32)
    scaled = (widened * gain).astype(jnp.bfloat16)
    local_squares = jnp.sum(widened * widened, axis=1)
    key_columns = key_weight.shape[1]
    weights = jnp.concatenate([key_weight, value_weight], axis=1)
    own_squares = total_squares(local_squares, local_tokens)
    projected = lax.psum_scatter(
        jnp.dot(scaled, weights, preferred_element_type=jnp.float32),
        "seq",
        scatter_dimension=0,
        tiled=True,
    )
    inverse_scale = lax.rsqrt(own_squares / D + EPSILON)
    projected = projected * inverse_scale[:, None]
    key_rows = rotary(projected[:, :key_columns].reshape(local_tokens, -1, HEAD_DIM), positions[0])
    value_rows = projected[:, key_columns:].reshape(local_tokens, -1, HEAD_DIM)
    joint_rows = (
        jnp.stack([key_rows, value_rows], axis=2).reshape(local_tokens, -1).astype(jnp.bfloat16)
    )
    tokens = local_tokens * lax.axis_size("seq") * lax.axis_size("batch")
    if tokens <= initial_basis.shape[0] * lax.axis_size("head"):
        own_rows = lax.all_gather(joint_rows, ("batch", "seq"), axis=0, tiled=True)
        joint_all = lax.all_gather(own_rows, "head", axis=1, tiled=True)
        return iterate(joint_all, whole_of(initial_basis), own_rows)
    partial_value = lax.dot_general(
        joint_rows,
        lax.all_gather(joint_rows, "head", axis=1, tiled=True),
        (((0,), (0,)), ((), ())),
        preferred_element_type=jnp.float32,
    )
    token_total = local_tokens * lax.axis_size("seq") * lax.axis_size("batch")
    basis_block = initial_basis
    covariance = lax.psum(partial_value, ("seq", "batch")) / token_total
    for iteration in range(ITERS):
        whole_basis = whole_of(basis_block)
        images = jnp.dot(
            covariance,
            whole_basis,
            precision=lax.Precision.HIGHEST,
            preferred_element_type=jnp.float32,
        )
        gram_matrix = lax.psum(gram_of(images), "head") / whole_basis.shape[0]
        basis_block = orthonormal(images, gram_matrix)
    return basis_block


def solution(mesh):
    return jax.shard_map(
        body,
        mesh=mesh,
        in_specs=(
            P("batch", None, "seq"),
            P("seq"),
            P("seq", "head"),
            P("seq", "head"),
            P("batch", "seq"),
            P("head", None),
        ),
        out_specs=P("head", None),
        check_vma=False,
    )
```

```python
import functools
import math

import jax
import jax.numpy as jnp
from jax import lax
from jax.experimental import pallas as pl
from jax.experimental.pallas import tpu as pltpu
from jax.sharding import PartitionSpec as P

D = 16384
HEAD_DIM = 128
ITERS = 4


EPSILON = 1e-05
ROTARY_BASE = 500000.0


def rotary(head_rows, position_row):
    half_width = head_rows.shape[-1] // 2
    index_row = jnp.arange(half_width, dtype=jnp.float32)
    frequency = jnp.exp(index_row * (-math.log(ROTARY_BASE) / half_width))
    angles = position_row.astype(jnp.float32)[:, None] * frequency[None, :]
    cosine = jnp.cos(angles)[:, None, :]
    sine_part = jnp.sin(angles)[:, None, :]
    first_half = head_rows[..., :half_width]
    second_half = head_rows[..., half_width:]
    return jnp.concatenate(
        [
            first_half * cosine - second_half * sine_part,
            second_half * cosine + first_half * sine_part,
        ],
        axis=-1,
    )


def whole_of(basis_block):
    return lax.all_gather(basis_block, "head", axis=0, tiled=True)


def total_squares(local_squares, local_tokens):
    all_squares = lax.psum(local_squares, "seq")
    return lax.dynamic_slice_in_dim(all_squares, lax.axis_index("seq") * local_tokens, local_tokens)


def gram_of(images):
    return lax.dot_general(
        images,
        images,
        (((0,), (0,)), ((), ())),
        precision=lax.Precision.HIGHEST,
        preferred_element_type=jnp.float32,
    )


def orthonormal(images, gram_matrix):
    factor = jnp.linalg.cholesky(gram_matrix)
    return lax.linalg.triangular_solve(
        factor, images, left_side=False, lower=True, transpose_a=True
    )


LANES = 128
SUBLANES = 8


def dot_of(left, right, left_axis, right_axis, precision=None):
    return lax.dot_general(
        left,
        right,
        (((left_axis,), (right_axis,)), ((), ())),
        precision=precision,
        preferred_element_type=jnp.float32,
    )


def exact(left, right, left_axis, right_axis):
    return dot_of(left, right, left_axis, right_axis, lax.Precision.HIGHEST)


def halves_of(value):
    high = value.astype(jnp.bfloat16)
    return high, (value - high.astype(jnp.float32)).astype(jnp.bfloat16)


def inverse_factor(matrix):
    size = matrix.shape[0]
    rows = lax.broadcasted_iota(jnp.int32, (SUBLANES, size), 0)
    lanes = lax.broadcasted_iota(jnp.int32, (SUBLANES, size), 1)
    groups = size // SUBLANES
    left = [matrix[SUBLANES * g : SUBLANES * (g + 1)] for g in range(groups)]
    right = [jnp.where(lanes == rows + SUBLANES * g, 1.0, 0.0) for g in range(groups)]
    done = []

    def spread_row(value, at):
        return jnp.broadcast_to(value[at : at + 1, :], (SUBLANES, size))

    def spread_lane(value, at):
        return jnp.broadcast_to(value[:, at : at + 1], (SUBLANES, size))

    for pivot in range(0, size, 2):
        own, at = pivot // SUBLANES, pivot % SUBLANES
        top, low = spread_row(left[own], at), spread_row(left[own], at + 1)
        top_right, low_right = spread_row(right[own], at), spread_row(right[own], at + 1)
        first, cross, last = (
            spread_lane(top, pivot),
            spread_lane(top, pivot + 1),
            spread_lane(low, pivot + 1),
        )
        scale = 1.0 / (first * last - cross * cross)
        mix_top = (top * last - low * cross) * scale
        mix_low = (low * first - top * cross) * scale
        mix_top_right = (top_right * last - low_right * cross) * scale
        mix_low_right = (low_right * first - top_right * cross) * scale
        ratio = cross / first
        done.append(
            (
                top_right * lax.rsqrt(first),
                (low_right - ratio * top_right) * lax.rsqrt(last - ratio * cross),
            )
        )
        for g in range(own, groups):
            if g == own and at + 2 >= SUBLANES:
                continue
            one, two = spread_lane(left[g], pivot), spread_lane(left[g], pivot + 1)
            if g == own:
                one = jnp.where(rows > at + 1, one, 0.0)
                two = jnp.where(rows > at + 1, two, 0.0)
            left[g] = left[g] - one * mix_top - two * mix_low
            right[g] = right[g] - one * mix_top_right - two * mix_low_right
    blocks = []
    for g in range(groups):
        block = jnp.zeros((SUBLANES, size), jnp.float32)
        for pair in range(SUBLANES // 2):
            upper, lower = done[g * SUBLANES // 2 + pair]
            block = jnp.where(rows == 2 * pair, upper, block)
            block = jnp.where(rows == 2 * pair + 1, lower, block)
        blocks.append(block)
    return jnp.concatenate(blocks, axis=0)


def iterate_kernel(
    joint_ref, basis_ref, out_ref, high_ref, low_ref, rows_ref, images_ref, gram_ref
):
    tokens, joint = joint_ref.shape
    rank = basis_ref.shape[1]
    panels = rank // LANES
    strip = 256
    for start in range(0, tokens, strip):
        kernel_rows = dot_of(joint_ref[start : start + strip, :], joint_ref[...], 1, 1) * (1.0 / tokens)
        high, low = halves_of(kernel_rows)
        high_ref[start : start + strip, :] = high
        low_ref[start : start + strip, :] = low
    basis_high, basis_low = halves_of(basis_ref[...])
    rows_ref[...] = dot_of(joint_ref[...], basis_high, 1, 0) + dot_of(joint_ref[...], basis_low, 1, 0)

    def step(iteration, carry):
        rows_high, rows_low = halves_of(rows_ref[...])
        images_ref[...] = (
            dot_of(high_ref[...], rows_high, 1, 0)
            + dot_of(high_ref[...], rows_low, 1, 0)
            + dot_of(low_ref[...], rows_high, 1, 0)
        )
        gram_ref[...] = exact(rows_ref[...], images_ref[...], 0, 0) * (1.0 / (tokens * joint))

        @pl.when(iteration < ITERS - 1)
        def _():
            rows_ref[...] = images_ref[...]

        def panel_step(panel, inner):
            at = pl.ds(pl.multiple_of(panel * LANES, LANES), LANES)
            inverse = inverse_factor(gram_ref[at, at])
            scaled = exact(inverse, gram_ref[at, :], 1, 0)
            lane = lax.broadcasted_iota(jnp.int32, scaled.shape, 1)
            scaled = jnp.where(lane >= (panel + 1) * LANES, scaled, 0.0)
            gram_ref[...] -= exact(scaled, scaled, 0, 0)
            columns = exact(rows_ref[:, at], inverse, 1, 1)
            rows_ref[...] -= exact(columns, scaled, 1, 0)
            rows_ref[:, at] = columns
            return inner

        lax.fori_loop(0, panels, panel_step, 0)
        return carry

    lax.fori_loop(0, ITERS, step, 0)
    rows_high, rows_low = halves_of(rows_ref[...])
    width = out_ref.shape[0]
    own = joint_ref[:, pl.ds(pl.multiple_of(lax.axis_index("head") * width, width), width)]
    out_ref[...] = (dot_of(own, rows_high, 0, 0) + dot_of(own, rows_low, 0, 0)) * (1.0 / tokens)


def iterate(joint_all, basis_all):
    tokens, joint = joint_all.shape
    rank = basis_all.shape[1]
    return pl.pallas_call(
        iterate_kernel,
        out_shape=jax.ShapeDtypeStruct((joint // lax.axis_size("head"), rank), jnp.float32),
        in_specs=[pl.BlockSpec(memory_space=pltpu.VMEM)] * 2,
        out_specs=pl.BlockSpec(memory_space=pltpu.VMEM),
        scratch_shapes=[
            pltpu.VMEM((tokens, tokens), jnp.bfloat16),
            pltpu.VMEM((tokens, tokens), jnp.bfloat16),
            pltpu.VMEM((tokens, rank), jnp.float32),
            pltpu.VMEM((tokens, rank), jnp.float32),
            pltpu.VMEM((rank, rank), jnp.float32),
        ],
        compiler_params=pltpu.CompilerParams(vmem_limit_bytes=40 * 2**20),
    )(joint_all, basis_all)


def project_kernel(hidden_ref, gain_ref, key_ref, value_ref, partial_ref, squares_ref):
    key_columns = key_ref.shape[1]

    @pl.when(pl.program_id(0) == 0)
    def _():
        partial_ref[...] = jnp.zeros_like(partial_ref)
        squares_ref[...] = jnp.zeros_like(squares_ref)

    widened = hidden_ref[...].astype(jnp.float32)
    scaled = (widened * gain_ref[...]).astype(jnp.bfloat16)
    partial_ref[:, :key_columns] += dot_of(scaled, key_ref[...], 1, 0)
    partial_ref[:, key_columns:] += dot_of(scaled, value_ref[...], 1, 0)
    squared = widened * widened
    total = squares_ref[...]
    for start in range(0, squared.shape[1], LANES):
        total = total + squared[:, start : start + LANES]
    squares_ref[...] = total


def project(hidden_rows, gain, key_weight, value_weight):
    tokens, depth = hidden_rows.shape
    key_columns, value_columns = key_weight.shape[1], value_weight.shape[1]
    chunk = math.gcd(depth, 1024)
    return pl.pallas_call(
        project_kernel,
        grid=(depth // chunk,),
        out_shape=(
            jax.ShapeDtypeStruct((tokens, key_columns + value_columns), jnp.float32),
            jax.ShapeDtypeStruct((tokens, LANES), jnp.float32),
        ),
        in_specs=[
            pl.BlockSpec((tokens, chunk), lambda step: (0, step)),
            pl.BlockSpec((1, chunk), lambda step: (0, step)),
            pl.BlockSpec((chunk, key_columns), lambda step: (step, 0)),
            pl.BlockSpec((chunk, value_columns), lambda step: (step, 0)),
        ],
        out_specs=(
            pl.BlockSpec((tokens, key_columns + value_columns), lambda step: (0, 0)),
            pl.BlockSpec((tokens, LANES), lambda step: (0, 0)),
        ),
        compiler_params=pltpu.CompilerParams(
            dimension_semantics=("arbitrary",), vmem_limit_bytes=60 * 2**20
        ),
    )(hidden_rows, gain[None, :], key_weight, value_weight)


def gather_kernel(
    heads,
    partial_ref,
    squares_ref,
    cosine_ref,
    sine_ref,
    out_ref,
    peer_partial,
    peer_squares,
    swap_sems,
    z_sems,
    x_sems,
    y_sems,
    x_half_sems,
    y_half_sems,
    core_sems,
):
    x, b, z = lax.axis_index("seq"), lax.axis_index("batch"), lax.axis_index("head")
    local, width = peer_partial.shape
    half = width // 2
    other_x, other_y = 1 - x, (b + 2) % 4
    partner = b + 1 - 2 * (b % 2)
    x_peer, y_peer, core_peer = (other_x, b, z), (x, other_y, z), (x, partner, z)

    def z_peer(d):
        return (x, b, (z + d) % heads)

    barrier = pltpu.get_barrier_semaphore()
    peers = [x_peer, y_peer, core_peer] + [z_peer(d) for d in range(1, heads)]
    for peer in peers:
        pl.semaphore_signal(barrier, inc=1, device_id=peer, device_id_type=pl.DeviceIdType.MESH)
    pl.semaphore_wait(barrier, len(peers))

    def copy(source, target, sems, peer):
        return pltpu.make_async_remote_copy(
            src_ref=source,
            dst_ref=target,
            send_sem=sems.at[0],
            recv_sem=sems.at[1],
            device_id=peer,
            device_id_type=pl.DeviceIdType.MESH,
        )

    def region(xs, bs, zs, start=0, size=width):
        row = pl.multiple_of((xs * 4 + bs) * local, local)
        column = pl.multiple_of(zs * width + start, half)
        return out_ref.at[pl.ds(row, local), pl.ds(column, size)]

    started = []

    def send(area, sems, peer):
        going = copy(area, area, sems, peer)
        going.start()
        started.append(going)

    def arrive(area, sems, peer):
        copy(area, area, sems, peer).wait_recv()

    away = pl.ds(pl.multiple_of(other_x * local, local), local)
    mine = pl.ds(pl.multiple_of(x * local, local), local)
    swaps = [
        copy(partial_ref.at[away, :], peer_partial, swap_sems.at[0], x_peer),
        copy(squares_ref.at[away, :], peer_squares, swap_sems.at[1], x_peer),
    ]
    for swap in swaps:
        swap.start()
    for swap in swaps:
        swap.wait()
    squares = jnp.sum(squares_ref[mine, :] + peer_squares[...], axis=1, keepdims=True)
    projected = (partial_ref[mine, :] + peer_partial[...]) * lax.rsqrt(squares / D + EPSILON)
    row = pl.multiple_of((x * 4 + b) * local, local)
    for g in range(half // HEAD_DIM):
        key = projected[:, g * HEAD_DIM : (g + 1) * HEAD_DIM]
        turned = key * cosine_ref[...] + pltpu.roll(key, HEAD_DIM // 2, 1) * sine_ref[...]
        value = projected[:, half + g * HEAD_DIM : half + (g + 1) * HEAD_DIM]
        column = pl.multiple_of(z * width + 2 * g * HEAD_DIM, HEAD_DIM)
        out_ref[pl.ds(row, local), pl.ds(column, HEAD_DIM)] = turned.astype(jnp.bfloat16)
        column = pl.multiple_of(z * width + (2 * g + 1) * HEAD_DIM, HEAD_DIM)
        out_ref[pl.ds(row, local), pl.ds(column, HEAD_DIM)] = value.astype(jnp.bfloat16)

    for d in range(1, heads):
        send(region(x, b, z), z_sems.at[d], z_peer(d))

    def source(d):
        return (z + heads - d) % heads

    def spread(d):
        area = region(x, b, source(d))
        if d:
            arrive(area, z_sems.at[d], z_peer(d))
        send(area, x_sems.at[d], x_peer)
        send(area, y_sems.at[d], y_peer)
        send(area, core_sems.at[d, 0], core_peer)

    def relay(d):
        s = source(d)
        arrive(region(other_x, b, s), x_sems.at[d], x_peer)
        send(region(other_x, b, s, half, half), y_half_sems.at[d], y_peer)
        send(region(other_x, b, s), core_sems.at[d, 1], core_peer)
        arrive(region(x, other_y, s), y_sems.at[d], y_peer)
        send(region(x, other_y, s, 0, half), x_half_sems.at[d], x_peer)
        send(region(x, other_y, s), core_sems.at[d, 2], core_peer)

    def finish(d):
        s = source(d)
        arrive(region(other_x, other_y, s, 0, half), x_half_sems.at[d], x_peer)
        arrive(region(other_x, other_y, s, half, half), y_half_sems.at[d], y_peer)
        send(region(other_x, other_y, s), core_sems.at[d, 3], core_peer)

    order = [0] + sorted(range(1, heads), key=lambda d: (min(d, heads - d), d))
    for turn in range(heads + 2):
        if turn < heads:
            spread(order[turn])
        if 1 <= turn < heads + 1:
            relay(order[turn - 1])
        if turn >= 2:
            finish(order[turn - 2])
    far = (partner + 2) % 4
    for d in order:
        s = source(d)
        areas = [(x, partner), (other_x, partner), (x, far), (other_x, far)]
        for kind, (xs, bs) in enumerate(areas):
            arrive(region(xs, bs, s), core_sems.at[d, kind], core_peer)
    for going in started:
        going.wait_send()


def gather(partial, squares, positions, heads, tokens):
    local, width = positions.shape[0], partial.shape[1]
    half_width = HEAD_DIM // 2
    frequency = jnp.exp(
        jnp.arange(half_width, dtype=jnp.float32) * (-math.log(ROTARY_BASE) / half_width)
    )
    angles = positions.astype(jnp.float32)[:, None] * frequency[None, :]
    cosine, sine = jnp.cos(angles), jnp.sin(angles)
    dma = pltpu.SemaphoreType.DMA
    return pl.pallas_call(
        functools.partial(gather_kernel, heads),
        out_shape=jax.ShapeDtypeStruct((tokens, heads * width), jnp.bfloat16),
        in_specs=[pl.BlockSpec(memory_space=pltpu.VMEM)] * 4,
        out_specs=pl.BlockSpec(memory_space=pltpu.VMEM),
        scratch_shapes=[
            pltpu.VMEM((local, width), jnp.float32),
            pltpu.VMEM((local, LANES), jnp.float32),
            dma((2, 2)),
            dma((heads, 2)),
            dma((heads, 2)),
            dma((heads, 2)),
            dma((heads, 2)),
            dma((heads, 2)),
            dma((heads, 4, 2)),
        ],
        compiler_params=pltpu.CompilerParams(
            collective_id=0, has_side_effects=True, vmem_limit_bytes=24 * 2**20
        ),
    )(
        partial,
        squares,
        jnp.concatenate([cosine, cosine], axis=1),
        jnp.concatenate([-sine, sine], axis=1),
    )


def body(hidden, gain, key_weight, value_weight, positions, initial_basis):
    hidden_rows = hidden[0]
    local_tokens = positions.shape[1]
    seqs, batches, heads = lax.axis_size("seq"), lax.axis_size("batch"), lax.axis_size("head")
    tokens = local_tokens * seqs * batches
    if seqs == 2 and batches == 4 and tokens <= initial_basis.shape[0] * heads:
        partial, squares = project(hidden_rows, gain, key_weight, value_weight)
        joint_all = gather(partial, squares, positions[0], heads, tokens)
        return iterate(joint_all, whole_of(initial_basis))
    widened = hidden_rows.astype(jnp.float32)
    scaled = (widened * gain).astype(jnp.bfloat16)
    local_squares = jnp.sum(widened * widened, axis=1)
    key_columns = key_weight.shape[1]
    weights = jnp.concatenate([key_weight, value_weight], axis=1)
    own_squares = total_squares(local_squares, local_tokens)
    projected = lax.psum_scatter(
        jnp.dot(scaled, weights, preferred_element_type=jnp.float32),
        "seq",
        scatter_dimension=0,
        tiled=True,
    )
    inverse_scale = lax.rsqrt(own_squares / D + EPSILON)
    projected = projected * inverse_scale[:, None]
    key_rows = rotary(projected[:, :key_columns].reshape(local_tokens, -1, HEAD_DIM), positions[0])
    value_rows = projected[:, key_columns:].reshape(local_tokens, -1, HEAD_DIM)
    joint_rows = (
        jnp.stack([key_rows, value_rows], axis=2).reshape(local_tokens, -1).astype(jnp.bfloat16)
    )
    partial_value = lax.dot_general(
        joint_rows,
        lax.all_gather(joint_rows, "head", axis=1, tiled=True),
        (((0,), (0,)), ((), ())),
        preferred_element_type=jnp.float32,
    )
    token_total = local_tokens * lax.axis_size("seq") * lax.axis_size("batch")
    basis_block = initial_basis
    covariance = lax.psum(partial_value, ("seq", "batch")) / token_total
    for iteration in range(ITERS):
        whole_basis = whole_of(basis_block)
        images = jnp.dot(
            covariance,
            whole_basis,
            precision=lax.Precision.HIGHEST,
            preferred_element_type=jnp.float32,
        )
        gram_matrix = lax.psum(gram_of(images), "head") / whole_basis.shape[0]
        basis_block = orthonormal(images, gram_matrix)
    return basis_block


def solution(mesh):
    return jax.shard_map(
        body,
        mesh=mesh,
        in_specs=(
            P("batch", None, "seq"),
            P("seq"),
            P("seq", "head"),
            P("seq", "head"),
            P("batch", "seq"),
            P("head", None),
        ),
        out_specs=P("head", None),
        check_vma=False,
    )
```

```python
import functools
import math

import jax
import jax.numpy as jnp
from jax import lax
from jax.experimental import pallas as pl
from jax.experimental.pallas import tpu as pltpu
from jax.sharding import PartitionSpec as P

D = 16384
HEAD_DIM = 128
ITERS = 4


EPSILON = 1e-05
ROTARY_BASE = 500000.0


def rotary(head_rows, position_row):
    half_width = head_rows.shape[-1] // 2
    index_row = jnp.arange(half_width, dtype=jnp.float32)
    frequency = jnp.exp(index_row * (-math.log(ROTARY_BASE) / half_width))
    angles = position_row.astype(jnp.float32)[:, None] * frequency[None, :]
    cosine = jnp.cos(angles)[:, None, :]
    sine_part = jnp.sin(angles)[:, None, :]
    first_half = head_rows[..., :half_width]
    second_half = head_rows[..., half_width:]
    return jnp.concatenate(
        [
            first_half * cosine - second_half * sine_part,
            second_half * cosine + first_half * sine_part,
        ],
        axis=-1,
    )


def whole_of(basis_block):
    return lax.all_gather(basis_block, "head", axis=0, tiled=True)


def total_squares(local_squares, local_tokens):
    all_squares = lax.psum(local_squares, "seq")
    return lax.dynamic_slice_in_dim(all_squares, lax.axis_index("seq") * local_tokens, local_tokens)


def gram_of(images):
    return lax.dot_general(
        images,
        images,
        (((0,), (0,)), ((), ())),
        precision=lax.Precision.HIGHEST,
        preferred_element_type=jnp.float32,
    )


def orthonormal(images, gram_matrix):
    factor = jnp.linalg.cholesky(gram_matrix)
    return lax.linalg.triangular_solve(
        factor, images, left_side=False, lower=True, transpose_a=True
    )


LANES = 128
SUBLANES = 8


def dot_of(left, right, left_axis, right_axis, precision=None):
    return lax.dot_general(
        left,
        right,
        (((left_axis,), (right_axis,)), ((), ())),
        precision=precision,
        preferred_element_type=jnp.float32,
    )


def exact(left, right, left_axis, right_axis):
    return dot_of(left, right, left_axis, right_axis, lax.Precision.HIGHEST)


def halves_of(value):
    high = value.astype(jnp.bfloat16)
    return high, (value - high.astype(jnp.float32)).astype(jnp.bfloat16)


def small_inverse(block):
    size = len(block)
    block = [list(line) for line in block]
    extra = [[None] * size for _ in range(size)]
    result = [[None] * size for _ in range(size)]

    def plus(left, right):
        return right if left is None else left if right is None else left + right

    def times(scale, value):
        return None if value is None else scale if isinstance(value, float) else scale * value

    def minus(left, right):
        return left if right is None else -right if left is None else left - right

    for i in range(size):
        extra[i][i] = 1.0
    for k in range(0, size, 2):
        first, cross, last = block[k][k], block[k + 1][k], block[k + 1][k + 1]
        scale = 1.0 / (first * last - cross * cross)
        for i in range(k + 2, size):
            one, two = block[i][k], block[i][k + 1]
            top = (one * last - two * cross) * scale
            low = (two * first - one * cross) * scale
            for j in range(k + 2, i + 1):
                block[i][j] = block[i][j] - (top * block[j][k] + low * block[j][k + 1])
            for j in range(k + 2):
                change = plus(times(top, extra[k][j]), times(low, extra[k + 1][j]))
                extra[i][j] = minus(extra[i][j], change)
        ratio = cross / first
        top_scale, low_scale = lax.rsqrt(first), lax.rsqrt(last - ratio * cross)
        for j in range(k + 2):
            result[k][j] = times(top_scale, extra[k][j])
            result[k + 1][j] = times(low_scale, minus(extra[k + 1][j], times(ratio, extra[k][j])))
    return result


def inverse_factor(matrix):
    size = matrix.shape[0]
    rows = lax.broadcasted_iota(jnp.int32, (SUBLANES, size), 0)
    lanes = lax.broadcasted_iota(jnp.int32, (SUBLANES, size), 1)
    groups = size // SUBLANES
    left = [matrix[SUBLANES * g : SUBLANES * (g + 1)] for g in range(groups)]
    right = [jnp.where(lanes == rows + SUBLANES * g, 1.0, 0.0) for g in range(groups)]

    def spread_row(value, at):
        return jnp.broadcast_to(value[at : at + 1, :], (SUBLANES, size))

    def spread_lane(value, at):
        return jnp.broadcast_to(value[:, at : at + 1], (SUBLANES, size))

    def stacked(values):
        total = jnp.zeros((SUBLANES, size), jnp.float32)
        for i, value in enumerate(values):
            if value is not None:
                total = jnp.where(rows == i, value, total)
        return total

    def combined(columns, value):
        terms = [columns[j] * spread_row(value, j) for j in range(SUBLANES)]
        while len(terms) > 1:
            terms = [terms[i] + terms[i + 1] for i in range(0, len(terms), 2)]
        return terms[0]

    for own in range(groups):
        pivot = own * SUBLANES
        tops = [spread_row(left[own], i) for i in range(SUBLANES)]
        block = [[spread_lane(tops[i], pivot + j) for j in range(i + 1)] for i in range(SUBLANES)]
        small = small_inverse(block)
        down = [stacked([small[i][j] for i in range(SUBLANES)]) for j in range(SUBLANES)]
        across = [stacked([small[j][i] for i in range(SUBLANES)]) for j in range(SUBLANES)]
        scaled_left, scaled_right = combined(down, left[own]), combined(down, right[own])
        right[own] = scaled_right
        if own + 1 == groups:
            break
        mixed_left, mixed_right = combined(across, scaled_left), combined(across, scaled_right)
        mixes = [
            (spread_row(mixed_left, j), spread_row(mixed_right, j)) for j in range(SUBLANES)
        ]
        for g in range(own + 1, groups):
            columns = [spread_lane(left[g], pivot + j) for j in range(SUBLANES)]
            for j in range(SUBLANES):
                left[g] = left[g] - columns[j] * mixes[j][0]
                right[g] = right[g] - columns[j] * mixes[j][1]
    return jnp.concatenate(right, axis=0)


def iterate_kernel(
    joint_ref, basis_ref, out_ref, high_ref, low_ref, rows_ref, images_ref, gram_ref
):
    tokens, joint = joint_ref.shape
    rank = basis_ref.shape[1]
    panels = rank // LANES
    strip = 256
    for start in range(0, tokens, strip):
        kernel_rows = dot_of(joint_ref[start : start + strip, :], joint_ref[...], 1, 1) * (1.0 / tokens)
        high, low = halves_of(kernel_rows)
        high_ref[start : start + strip, :] = high
        low_ref[start : start + strip, :] = low
    basis_high, basis_low = halves_of(basis_ref[...])
    rows_ref[...] = dot_of(joint_ref[...], basis_high, 1, 0) + dot_of(joint_ref[...], basis_low, 1, 0)

    def step(iteration, carry):
        rows_high, rows_low = halves_of(rows_ref[...])
        images_ref[...] = (
            dot_of(high_ref[...], rows_high, 1, 0)
            + dot_of(high_ref[...], rows_low, 1, 0)
            + dot_of(low_ref[...], rows_high, 1, 0)
        )
        gram_ref[...] = exact(rows_ref[...], images_ref[...], 0, 0) * (1.0 / (tokens * joint))

        @pl.when(iteration < ITERS - 1)
        def _():
            rows_ref[...] = images_ref[...]

        def panel_step(panel, inner):
            at = pl.ds(pl.multiple_of(panel * LANES, LANES), LANES)
            inverse = inverse_factor(gram_ref[at, at])
            scaled = exact(inverse, gram_ref[at, :], 1, 0)
            lane = lax.broadcasted_iota(jnp.int32, scaled.shape, 1)
            scaled = jnp.where(lane >= (panel + 1) * LANES, scaled, 0.0)
            gram_ref[...] -= exact(scaled, scaled, 0, 0)
            columns = exact(rows_ref[:, at], inverse, 1, 1)
            rows_ref[...] -= exact(columns, scaled, 1, 0)
            rows_ref[:, at] = columns
            return inner

        lax.fori_loop(0, panels, panel_step, 0)
        return carry

    lax.fori_loop(0, ITERS, step, 0)
    rows_high, rows_low = halves_of(rows_ref[...])
    width = out_ref.shape[0]
    own = joint_ref[:, pl.ds(pl.multiple_of(lax.axis_index("head") * width, width), width)]
    out_ref[...] = (dot_of(own, rows_high, 0, 0) + dot_of(own, rows_low, 0, 0)) * (1.0 / tokens)


def iterate(joint_all, basis_all):
    tokens, joint = joint_all.shape
    rank = basis_all.shape[1]
    return pl.pallas_call(
        iterate_kernel,
        out_shape=jax.ShapeDtypeStruct((joint // lax.axis_size("head"), rank), jnp.float32),
        in_specs=[pl.BlockSpec(memory_space=pltpu.VMEM)] * 2,
        out_specs=pl.BlockSpec(memory_space=pltpu.VMEM),
        scratch_shapes=[
            pltpu.VMEM((tokens, tokens), jnp.bfloat16),
            pltpu.VMEM((tokens, tokens), jnp.bfloat16),
            pltpu.VMEM((tokens, rank), jnp.float32),
            pltpu.VMEM((tokens, rank), jnp.float32),
            pltpu.VMEM((rank, rank), jnp.float32),
        ],
        compiler_params=pltpu.CompilerParams(vmem_limit_bytes=40 * 2**20),
    )(joint_all, basis_all)


def project_kernel(hidden_ref, gain_ref, key_ref, value_ref, partial_ref, squares_ref):
    key_columns = key_ref.shape[1]

    @pl.when(pl.program_id(0) == 0)
    def _():
        partial_ref[...] = jnp.zeros_like(partial_ref)
        squares_ref[...] = jnp.zeros_like(squares_ref)

    widened = hidden_ref[...].astype(jnp.float32)
    scaled = (widened * gain_ref[...]).astype(jnp.bfloat16)
    partial_ref[:, :key_columns] += dot_of(scaled, key_ref[...], 1, 0)
    partial_ref[:, key_columns:] += dot_of(scaled, value_ref[...], 1, 0)
    squared = widened * widened
    total = squares_ref[...]
    for start in range(0, squared.shape[1], LANES):
        total = total + squared[:, start : start + LANES]
    squares_ref[...] = total


def project(hidden_rows, gain, key_weight, value_weight):
    tokens, depth = hidden_rows.shape
    key_columns, value_columns = key_weight.shape[1], value_weight.shape[1]
    chunk = math.gcd(depth, 1024)
    return pl.pallas_call(
        project_kernel,
        grid=(depth // chunk,),
        out_shape=(
            jax.ShapeDtypeStruct((tokens, key_columns + value_columns), jnp.float32),
            jax.ShapeDtypeStruct((tokens, LANES), jnp.float32),
        ),
        in_specs=[
            pl.BlockSpec((tokens, chunk), lambda step: (0, step)),
            pl.BlockSpec((1, chunk), lambda step: (0, step)),
            pl.BlockSpec((chunk, key_columns), lambda step: (step, 0)),
            pl.BlockSpec((chunk, value_columns), lambda step: (step, 0)),
        ],
        out_specs=(
            pl.BlockSpec((tokens, key_columns + value_columns), lambda step: (0, 0)),
            pl.BlockSpec((tokens, LANES), lambda step: (0, 0)),
        ),
        compiler_params=pltpu.CompilerParams(
            dimension_semantics=("arbitrary",), vmem_limit_bytes=60 * 2**20
        ),
    )(hidden_rows, gain[None, :], key_weight, value_weight)


def gather_kernel(
    heads,
    partial_ref,
    squares_ref,
    cosine_ref,
    sine_ref,
    out_ref,
    peer_partial,
    peer_squares,
    swap_sems,
    z_sems,
    x_sems,
    y_sems,
    x_half_sems,
    y_half_sems,
    core_sems,
):
    x, b, z = lax.axis_index("seq"), lax.axis_index("batch"), lax.axis_index("head")
    local, width = peer_partial.shape
    half = width // 2
    other_x, other_y = 1 - x, (b + 2) % 4
    partner = b + 1 - 2 * (b % 2)
    x_peer, y_peer, core_peer = (other_x, b, z), (x, other_y, z), (x, partner, z)

    def z_peer(d):
        return (x, b, (z + d) % heads)

    barrier = pltpu.get_barrier_semaphore()
    peers = [x_peer, y_peer, core_peer] + [z_peer(d) for d in range(1, heads)]
    for peer in peers:
        pl.semaphore_signal(barrier, inc=1, device_id=peer, device_id_type=pl.DeviceIdType.MESH)
    pl.semaphore_wait(barrier, len(peers))

    def copy(source, target, sems, peer):
        return pltpu.make_async_remote_copy(
            src_ref=source,
            dst_ref=target,
            send_sem=sems.at[0],
            recv_sem=sems.at[1],
            device_id=peer,
            device_id_type=pl.DeviceIdType.MESH,
        )

    def region(xs, bs, zs, start=0, size=width):
        row = pl.multiple_of((xs * 4 + bs) * local, local)
        column = pl.multiple_of(zs * width + start, half)
        return out_ref.at[pl.ds(row, local), pl.ds(column, size)]

    started = []

    def send(area, sems, peer):
        going = copy(area, area, sems, peer)
        going.start()
        started.append(going)

    def arrive(area, sems, peer):
        copy(area, area, sems, peer).wait_recv()

    away = pl.ds(pl.multiple_of(other_x * local, local), local)
    mine = pl.ds(pl.multiple_of(x * local, local), local)
    swaps = [
        copy(partial_ref.at[away, :], peer_partial, swap_sems.at[0], x_peer),
        copy(squares_ref.at[away, :], peer_squares, swap_sems.at[1], x_peer),
    ]
    for swap in swaps:
        swap.start()
    for swap in swaps:
        swap.wait()
    squares = jnp.sum(squares_ref[mine, :] + peer_squares[...], axis=1, keepdims=True)
    projected = (partial_ref[mine, :] + peer_partial[...]) * lax.rsqrt(squares / D + EPSILON)
    row = pl.multiple_of((x * 4 + b) * local, local)
    for g in range(half // HEAD_DIM):
        key = projected[:, g * HEAD_DIM : (g + 1) * HEAD_DIM]
        turned = key * cosine_ref[...] + pltpu.roll(key, HEAD_DIM // 2, 1) * sine_ref[...]
        value = projected[:, half + g * HEAD_DIM : half + (g + 1) * HEAD_DIM]
        column = pl.multiple_of(z * width + 2 * g * HEAD_DIM, HEAD_DIM)
        out_ref[pl.ds(row, local), pl.ds(column, HEAD_DIM)] = turned.astype(jnp.bfloat16)
        column = pl.multiple_of(z * width + (2 * g + 1) * HEAD_DIM, HEAD_DIM)
        out_ref[pl.ds(row, local), pl.ds(column, HEAD_DIM)] = value.astype(jnp.bfloat16)

    for d in range(1, heads):
        send(region(x, b, z), z_sems.at[d], z_peer(d))

    def source(d):
        return (z + heads - d) % heads

    def spread(d):
        area = region(x, b, source(d))
        if d:
            arrive(area, z_sems.at[d], z_peer(d))
        send(area, x_sems.at[d], x_peer)
        send(area, y_sems.at[d], y_peer)
        send(area, core_sems.at[d, 0], core_peer)

    def relay(d):
        s = source(d)
        arrive(region(other_x, b, s), x_sems.at[d], x_peer)
        send(region(other_x, b, s, half, half), y_half_sems.at[d], y_peer)
        send(region(other_x, b, s), core_sems.at[d, 1], core_peer)
        arrive(region(x, other_y, s), y_sems.at[d], y_peer)
        send(region(x, other_y, s, 0, half), x_half_sems.at[d], x_peer)
        send(region(x, other_y, s), core_sems.at[d, 2], core_peer)

    def finish(d):
        s = source(d)
        arrive(region(other_x, other_y, s, 0, half), x_half_sems.at[d], x_peer)
        arrive(region(other_x, other_y, s, half, half), y_half_sems.at[d], y_peer)
        send(region(other_x, other_y, s), core_sems.at[d, 3], core_peer)

    order = [0] + sorted(range(1, heads), key=lambda d: (min(d, heads - d), d))
    for turn in range(heads + 2):
        if turn < heads:
            spread(order[turn])
        if 1 <= turn < heads + 1:
            relay(order[turn - 1])
        if turn >= 2:
            finish(order[turn - 2])
    far = (partner + 2) % 4
    for d in order:
        s = source(d)
        areas = [(x, partner), (other_x, partner), (x, far), (other_x, far)]
        for kind, (xs, bs) in enumerate(areas):
            arrive(region(xs, bs, s), core_sems.at[d, kind], core_peer)
    for going in started:
        going.wait_send()


def gather(partial, squares, positions, heads, tokens):
    local, width = positions.shape[0], partial.shape[1]
    half_width = HEAD_DIM // 2
    frequency = jnp.exp(
        jnp.arange(half_width, dtype=jnp.float32) * (-math.log(ROTARY_BASE) / half_width)
    )
    angles = positions.astype(jnp.float32)[:, None] * frequency[None, :]
    cosine, sine = jnp.cos(angles), jnp.sin(angles)
    dma = pltpu.SemaphoreType.DMA
    return pl.pallas_call(
        functools.partial(gather_kernel, heads),
        out_shape=jax.ShapeDtypeStruct((tokens, heads * width), jnp.bfloat16),
        in_specs=[pl.BlockSpec(memory_space=pltpu.VMEM)] * 4,
        out_specs=pl.BlockSpec(memory_space=pltpu.VMEM),
        scratch_shapes=[
            pltpu.VMEM((local, width), jnp.float32),
            pltpu.VMEM((local, LANES), jnp.float32),
            dma((2, 2)),
            dma((heads, 2)),
            dma((heads, 2)),
            dma((heads, 2)),
            dma((heads, 2)),
            dma((heads, 2)),
            dma((heads, 4, 2)),
        ],
        compiler_params=pltpu.CompilerParams(
            collective_id=0, has_side_effects=True, vmem_limit_bytes=24 * 2**20
        ),
    )(
        partial,
        squares,
        jnp.concatenate([cosine, cosine], axis=1),
        jnp.concatenate([-sine, sine], axis=1),
    )


def body(hidden, gain, key_weight, value_weight, positions, initial_basis):
    hidden_rows = hidden[0]
    local_tokens = positions.shape[1]
    seqs, batches, heads = lax.axis_size("seq"), lax.axis_size("batch"), lax.axis_size("head")
    tokens = local_tokens * seqs * batches
    if seqs == 2 and batches == 4 and tokens <= initial_basis.shape[0] * heads:
        partial, squares = project(hidden_rows, gain, key_weight, value_weight)
        joint_all = gather(partial, squares, positions[0], heads, tokens)
        return iterate(joint_all, whole_of(initial_basis))
    widened = hidden_rows.astype(jnp.float32)
    scaled = (widened * gain).astype(jnp.bfloat16)
    local_squares = jnp.sum(widened * widened, axis=1)
    key_columns = key_weight.shape[1]
    weights = jnp.concatenate([key_weight, value_weight], axis=1)
    own_squares = total_squares(local_squares, local_tokens)
    projected = lax.psum_scatter(
        jnp.dot(scaled, weights, preferred_element_type=jnp.float32),
        "seq",
        scatter_dimension=0,
        tiled=True,
    )
    inverse_scale = lax.rsqrt(own_squares / D + EPSILON)
    projected = projected * inverse_scale[:, None]
    key_rows = rotary(projected[:, :key_columns].reshape(local_tokens, -1, HEAD_DIM), positions[0])
    value_rows = projected[:, key_columns:].reshape(local_tokens, -1, HEAD_DIM)
    joint_rows = (
        jnp.stack([key_rows, value_rows], axis=2).reshape(local_tokens, -1).astype(jnp.bfloat16)
    )
    partial_value = lax.dot_general(
        joint_rows,
        lax.all_gather(joint_rows, "head", axis=1, tiled=True),
        (((0,), (0,)), ((), ())),
        preferred_element_type=jnp.float32,
    )
    token_total = local_tokens * lax.axis_size("seq") * lax.axis_size("batch")
    basis_block = initial_basis
    covariance = lax.psum(partial_value, ("seq", "batch")) / token_total
    for iteration in range(ITERS):
        whole_basis = whole_of(basis_block)
        images = jnp.dot(
            covariance,
            whole_basis,
            precision=lax.Precision.HIGHEST,
            preferred_element_type=jnp.float32,
        )
        gram_matrix = lax.psum(gram_of(images), "head") / whole_basis.shape[0]
        basis_block = orthonormal(images, gram_matrix)
    return basis_block


def solution(mesh):
    return jax.shard_map(
        body,
        mesh=mesh,
        in_specs=(
            P("batch", None, "seq"),
            P("seq"),
            P("seq", "head"),
            P("seq", "head"),
            P("batch", "seq"),
            P("head", None),
        ),
        out_specs=P("head", None),
        check_vma=False,
    )
```

```python
import functools
import math

import jax
import jax.numpy as jnp
from jax import lax
from jax.experimental import pallas as pl
from jax.experimental.pallas import tpu as pltpu
from jax.sharding import PartitionSpec as P

D = 16384
HEAD_DIM = 128
ITERS = 4


EPSILON = 1e-05
ROTARY_BASE = 500000.0


def rotary(head_rows, position_row):
    half_width = head_rows.shape[-1] // 2
    index_row = jnp.arange(half_width, dtype=jnp.float32)
    frequency = jnp.exp(index_row * (-math.log(ROTARY_BASE) / half_width))
    angles = position_row.astype(jnp.float32)[:, None] * frequency[None, :]
    cosine = jnp.cos(angles)[:, None, :]
    sine_part = jnp.sin(angles)[:, None, :]
    first_half = head_rows[..., :half_width]
    second_half = head_rows[..., half_width:]
    return jnp.concatenate(
        [
            first_half * cosine - second_half * sine_part,
            second_half * cosine + first_half * sine_part,
        ],
        axis=-1,
    )


def whole_of(basis_block):
    return lax.all_gather(basis_block, "head", axis=0, tiled=True)


def total_squares(local_squares, local_tokens):
    all_squares = lax.psum(local_squares, "seq")
    return lax.dynamic_slice_in_dim(all_squares, lax.axis_index("seq") * local_tokens, local_tokens)


def gram_of(images):
    return lax.dot_general(
        images,
        images,
        (((0,), (0,)), ((), ())),
        precision=lax.Precision.HIGHEST,
        preferred_element_type=jnp.float32,
    )


def orthonormal(images, gram_matrix):
    factor = jnp.linalg.cholesky(gram_matrix)
    return lax.linalg.triangular_solve(
        factor, images, left_side=False, lower=True, transpose_a=True
    )


LANES = 128
SUBLANES = 8


def dot_of(left, right, left_axis, right_axis, precision=None):
    return lax.dot_general(
        left,
        right,
        (((left_axis,), (right_axis,)), ((), ())),
        precision=precision,
        preferred_element_type=jnp.float32,
    )


def exact(left, right, left_axis, right_axis):
    return dot_of(left, right, left_axis, right_axis, lax.Precision.HIGHEST)


def halves_of(value):
    high = value.astype(jnp.bfloat16)
    return high, (value - high.astype(jnp.float32)).astype(jnp.bfloat16)


def small_inverse(block):
    size = len(block)
    block = [list(line) for line in block]
    extra = [[None] * size for _ in range(size)]
    result = [[None] * size for _ in range(size)]

    def plus(left, right):
        return right if left is None else left if right is None else left + right

    def times(scale, value):
        return None if value is None else scale if isinstance(value, float) else scale * value

    def minus(left, right):
        return left if right is None else -right if left is None else left - right

    for i in range(size):
        extra[i][i] = 1.0
    for k in range(0, size, 2):
        first, cross, last = block[k][k], block[k + 1][k], block[k + 1][k + 1]
        scale = 1.0 / (first * last - cross * cross)
        for i in range(k + 2, size):
            one, two = block[i][k], block[i][k + 1]
            top = (one * last - two * cross) * scale
            low = (two * first - one * cross) * scale
            for j in range(k + 2, i + 1):
                block[i][j] = block[i][j] - (top * block[j][k] + low * block[j][k + 1])
            for j in range(k + 2):
                change = plus(times(top, extra[k][j]), times(low, extra[k + 1][j]))
                extra[i][j] = minus(extra[i][j], change)
        ratio = cross / first
        top_scale, low_scale = lax.rsqrt(first), lax.rsqrt(last - ratio * cross)
        for j in range(k + 2):
            result[k][j] = times(top_scale, extra[k][j])
            result[k + 1][j] = times(low_scale, minus(extra[k + 1][j], times(ratio, extra[k][j])))
    return result


def inverse_factor(matrix):
    size = matrix.shape[0]
    rows = lax.broadcasted_iota(jnp.int32, (SUBLANES, size), 0)
    lanes = lax.broadcasted_iota(jnp.int32, (SUBLANES, size), 1)
    groups = size // SUBLANES
    left = [matrix[SUBLANES * g : SUBLANES * (g + 1)] for g in range(groups)]
    right = [jnp.where(lanes == rows + SUBLANES * g, 1.0, 0.0) for g in range(groups)]

    def spread_row(value, at):
        return jnp.broadcast_to(value[at : at + 1, :], (SUBLANES, size))

    def spread_lane(value, at):
        return jnp.broadcast_to(value[:, at : at + 1], (SUBLANES, size))

    def stacked(values):
        total = jnp.zeros((SUBLANES, size), jnp.float32)
        for i, value in enumerate(values):
            if value is not None:
                total = jnp.where(rows == i, value, total)
        return total

    def combined(columns, value):
        terms = [columns[j] * spread_row(value, j) for j in range(SUBLANES)]
        while len(terms) > 1:
            terms = [terms[i] + terms[i + 1] for i in range(0, len(terms), 2)]
        return terms[0]

    for own in range(groups):
        pivot = own * SUBLANES
        tops = [spread_row(left[own], i) for i in range(SUBLANES)]
        block = [[spread_lane(tops[i], pivot + j) for j in range(i + 1)] for i in range(SUBLANES)]
        small = small_inverse(block)
        down = [stacked([small[i][j] for i in range(SUBLANES)]) for j in range(SUBLANES)]
        across = [stacked([small[j][i] for i in range(SUBLANES)]) for j in range(SUBLANES)]
        scaled_left, scaled_right = combined(down, left[own]), combined(down, right[own])
        right[own] = scaled_right
        if own + 1 == groups:
            break
        mixed_left, mixed_right = combined(across, scaled_left), combined(across, scaled_right)
        mixes = [
            (spread_row(mixed_left, j), spread_row(mixed_right, j)) for j in range(SUBLANES)
        ]
        for g in range(own + 1, groups):
            columns = [spread_lane(left[g], pivot + j) for j in range(SUBLANES)]
            for j in range(SUBLANES):
                left[g] = left[g] - columns[j] * mixes[j][0]
                right[g] = right[g] - columns[j] * mixes[j][1]
    return jnp.concatenate(right, axis=0)


def iterate_kernel(
    joint_ref, basis_ref, out_ref, high_ref, low_ref, rows_ref, images_ref, gram_ref
):
    tokens, joint = joint_ref.shape
    rank = basis_ref.shape[1]
    panels = rank // LANES
    strip = 256
    for start in range(0, tokens, strip):
        kernel_rows = dot_of(joint_ref[start : start + strip, :], joint_ref[...], 1, 1) * (1.0 / tokens)
        high, low = halves_of(kernel_rows)
        high_ref[start : start + strip, :] = high
        low_ref[start : start + strip, :] = low
    basis_high, basis_low = halves_of(basis_ref[...])
    rows_ref[...] = dot_of(joint_ref[...], basis_high, 1, 0) + dot_of(joint_ref[...], basis_low, 1, 0)

    def step(iteration, carry):
        rows_high, rows_low = halves_of(rows_ref[...])
        images_ref[...] = (
            dot_of(high_ref[...], rows_high, 1, 0)
            + dot_of(high_ref[...], rows_low, 1, 0)
            + dot_of(low_ref[...], rows_high, 1, 0)
        )
        gram_ref[...] = exact(rows_ref[...], images_ref[...], 0, 0) * (1.0 / (tokens * joint))

        @pl.when(iteration < ITERS - 1)
        def _():
            rows_ref[...] = images_ref[...]

        def panel_step(panel, inner):
            at = pl.ds(pl.multiple_of(panel * LANES, LANES), LANES)
            inverse = inverse_factor(gram_ref[at, at])
            scaled = exact(inverse, gram_ref[at, :], 1, 0)
            lane = lax.broadcasted_iota(jnp.int32, scaled.shape, 1)
            scaled = jnp.where(lane >= (panel + 1) * LANES, scaled, 0.0)
            gram_ref[...] -= exact(scaled, scaled, 0, 0)
            columns = exact(rows_ref[:, at], inverse, 1, 1)
            rows_ref[...] -= exact(columns, scaled, 1, 0)
            rows_ref[:, at] = columns
            return inner

        lax.fori_loop(0, panels, panel_step, 0)
        return carry

    lax.fori_loop(0, ITERS, step, 0)
    rows_high, rows_low = halves_of(rows_ref[...])
    width = out_ref.shape[0]
    own = joint_ref[:, pl.ds(pl.multiple_of(lax.axis_index("head") * width, width), width)]
    out_ref[...] = (dot_of(own, rows_high, 0, 0) + dot_of(own, rows_low, 0, 0)) * (1.0 / tokens)


def iterate(joint_all, basis_all):
    tokens, joint = joint_all.shape
    rank = basis_all.shape[1]
    return pl.pallas_call(
        iterate_kernel,
        out_shape=jax.ShapeDtypeStruct((joint // lax.axis_size("head"), rank), jnp.float32),
        in_specs=[pl.BlockSpec(memory_space=pltpu.VMEM)] * 2,
        out_specs=pl.BlockSpec(memory_space=pltpu.VMEM),
        scratch_shapes=[
            pltpu.VMEM((tokens, tokens), jnp.bfloat16),
            pltpu.VMEM((tokens, tokens), jnp.bfloat16),
            pltpu.VMEM((tokens, rank), jnp.float32),
            pltpu.VMEM((tokens, rank), jnp.float32),
            pltpu.VMEM((rank, rank), jnp.float32),
        ],
        compiler_params=pltpu.CompilerParams(vmem_limit_bytes=40 * 2**20),
    )(joint_all, basis_all)


def project_kernel(hidden_ref, gain_ref, key_ref, value_ref, partial_ref, squares_ref):
    key_columns = key_ref.shape[1]

    @pl.when(pl.program_id(0) == 0)
    def _():
        partial_ref[...] = jnp.zeros_like(partial_ref)
        squares_ref[...] = jnp.zeros_like(squares_ref)

    widened = hidden_ref[...].astype(jnp.float32)
    scaled = (widened * gain_ref[...]).astype(jnp.bfloat16)
    partial_ref[:, :key_columns] += dot_of(scaled, key_ref[...], 1, 0)
    partial_ref[:, key_columns:] += dot_of(scaled, value_ref[...], 1, 0)
    squared = widened * widened
    total = squares_ref[...]
    for start in range(0, squared.shape[1], LANES):
        total = total + squared[:, start : start + LANES]
    squares_ref[...] = total


def project(hidden_rows, gain, key_weight, value_weight):
    tokens, depth = hidden_rows.shape
    key_columns, value_columns = key_weight.shape[1], value_weight.shape[1]
    chunk = math.gcd(depth, 1024)
    return pl.pallas_call(
        project_kernel,
        grid=(depth // chunk,),
        out_shape=(
            jax.ShapeDtypeStruct((tokens, key_columns + value_columns), jnp.float32),
            jax.ShapeDtypeStruct((tokens, LANES), jnp.float32),
        ),
        in_specs=[
            pl.BlockSpec((tokens, chunk), lambda step: (0, step)),
            pl.BlockSpec((1, chunk), lambda step: (0, step)),
            pl.BlockSpec((chunk, key_columns), lambda step: (step, 0)),
            pl.BlockSpec((chunk, value_columns), lambda step: (step, 0)),
        ],
        out_specs=(
            pl.BlockSpec((tokens, key_columns + value_columns), lambda step: (0, 0)),
            pl.BlockSpec((tokens, LANES), lambda step: (0, 0)),
        ),
        compiler_params=pltpu.CompilerParams(
            dimension_semantics=("arbitrary",), vmem_limit_bytes=60 * 2**20
        ),
    )(hidden_rows, gain[None, :], key_weight, value_weight)


def gather_kernel(
    heads,
    partial_ref,
    squares_ref,
    cosine_ref,
    sine_ref,
    basis_ref,
    out_ref,
    whole_ref,
    peer_partial,
    peer_squares,
    swap_sems,
    z_sems,
    x_sems,
    y_sems,
    x_half_sems,
    y_half_sems,
    core_sems,
):
    x, b, z = lax.axis_index("seq"), lax.axis_index("batch"), lax.axis_index("head")
    local, width = peer_partial.shape
    half = width // 2
    rank = basis_ref.shape[1]
    piece = width // 8
    other_x, other_y = 1 - x, (b + 2) % 4
    partner = b + 1 - 2 * (b % 2)
    x_peer, y_peer, core_peer = (other_x, b, z), (x, other_y, z), (x, partner, z)

    def z_peer(d):
        return (x, b, (z + d) % heads)

    barrier = pltpu.get_barrier_semaphore()
    peers = [x_peer, y_peer, core_peer] + [z_peer(d) for d in range(1, heads)]
    for peer in peers:
        pl.semaphore_signal(barrier, inc=1, device_id=peer, device_id_type=pl.DeviceIdType.MESH)
    pl.semaphore_wait(barrier, len(peers))

    def copy(source, target, sems, peer):
        return pltpu.make_async_remote_copy(
            src_ref=source,
            dst_ref=target,
            send_sem=sems.at[0],
            recv_sem=sems.at[1],
            device_id=peer,
            device_id_type=pl.DeviceIdType.MESH,
        )

    def region(xs, bs, zs, start=0, size=width):
        row = pl.multiple_of((xs * 4 + bs) * local, local)
        column = pl.multiple_of(zs * width + start, half)
        return out_ref.at[pl.ds(row, local), pl.ds(column, size)]

    def piece_of(xs, bs, zs, start=0, size=rank):
        row = pl.multiple_of(zs * width + (xs * 4 + bs) * piece, piece)
        return whole_ref.at[pl.ds(row, piece), pl.ds(start, size)]

    started = []

    def send(area, sems, peer):
        going = copy(area, area, sems, peer)
        going.start()
        started.append(going)

    def arrive(area, sems, peer):
        copy(area, area, sems, peer).wait_recv()

    def source(d):
        return (z + heads - d) % heads

    order = [0] + sorted(range(1, heads), key=lambda d: (min(d, heads - d), d))
    own_piece = basis_ref.at[pl.ds(pl.multiple_of((x * 4 + b) * piece, piece), piece), :]
    for d in range(1, heads):
        going = copy(own_piece, piece_of(x, b, z), z_sems.at[1, d], z_peer(d))
        going.start()
        started.append(going)

    away = pl.ds(pl.multiple_of(other_x * local, local), local)
    mine = pl.ds(pl.multiple_of(x * local, local), local)
    swaps = [
        copy(partial_ref.at[away, :], peer_partial, swap_sems.at[0], x_peer),
        copy(squares_ref.at[away, :], peer_squares, swap_sems.at[1], x_peer),
    ]
    for swap in swaps:
        swap.start()
    whole_ref[pl.ds(pl.multiple_of(z * width, width), width), :] = basis_ref[...]
    for swap in swaps:
        swap.wait()
    squares = jnp.sum(squares_ref[mine, :] + peer_squares[...], axis=1, keepdims=True)
    projected = (partial_ref[mine, :] + peer_partial[...]) * lax.rsqrt(squares / D + EPSILON)
    row = pl.multiple_of((x * 4 + b) * local, local)
    for g in range(half // HEAD_DIM):
        key = projected[:, g * HEAD_DIM : (g + 1) * HEAD_DIM]
        turned = key * cosine_ref[...] + pltpu.roll(key, HEAD_DIM // 2, 1) * sine_ref[...]
        value = projected[:, half + g * HEAD_DIM : half + (g + 1) * HEAD_DIM]
        column = pl.multiple_of(z * width + 2 * g * HEAD_DIM, HEAD_DIM)
        out_ref[pl.ds(row, local), pl.ds(column, HEAD_DIM)] = turned.astype(jnp.bfloat16)
        column = pl.multiple_of(z * width + (2 * g + 1) * HEAD_DIM, HEAD_DIM)
        out_ref[pl.ds(row, local), pl.ds(column, HEAD_DIM)] = value.astype(jnp.bfloat16)

    for d in range(1, heads):
        send(region(x, b, z), z_sems.at[0, d], z_peer(d))

    def spread(kind, area, middle, d):
        mine = area(x, b, source(d))
        if d:
            arrive(mine, z_sems.at[kind, d], z_peer(d))
        send(mine, x_sems.at[kind, d], x_peer)
        send(mine, y_sems.at[kind, d], y_peer)
        send(mine, core_sems.at[kind, d, 0], core_peer)

    def relay(kind, area, middle, d):
        s = source(d)
        arrive(area(other_x, b, s), x_sems.at[kind, d], x_peer)
        send(area(other_x, b, s, middle, middle), y_half_sems.at[kind, d], y_peer)
        send(area(other_x, b, s), core_sems.at[kind, d, 1], core_peer)
        arrive(area(x, other_y, s), y_sems.at[kind, d], y_peer)
        send(area(x, other_y, s, 0, middle), x_half_sems.at[kind, d], x_peer)
        send(area(x, other_y, s), core_sems.at[kind, d, 2], core_peer)

    def finish(kind, area, middle, d):
        s = source(d)
        arrive(area(other_x, other_y, s, 0, middle), x_half_sems.at[kind, d], x_peer)
        arrive(area(other_x, other_y, s, middle, middle), y_half_sems.at[kind, d], y_peer)
        send(area(other_x, other_y, s), core_sems.at[kind, d, 3], core_peer)

    joint, pieces = (0, region, half), (1, piece_of, rank // 2)
    items = [joint + (0,)] + [pieces + (d,) for d in order[1:]] + [joint + (d,) for d in order[1:]]
    for turn in range(len(items) + 2):
        if turn < len(items):
            spread(*items[turn])
        if 1 <= turn < len(items) + 1:
            relay(*items[turn - 1])
        if turn >= 2:
            finish(*items[turn - 2])
    far = (partner + 2) % 4
    for kind, area, middle, d in items:
        s = source(d)
        places = [(x, partner), (other_x, partner), (x, far), (other_x, far)]
        for place, (xs, bs) in enumerate(places):
            arrive(area(xs, bs, s), core_sems.at[kind, d, place], core_peer)
    for going in started:
        going.wait_send()


def gather(partial, squares, positions, basis, heads, tokens):
    local, width = positions.shape[0], partial.shape[1]
    half_width = HEAD_DIM // 2
    frequency = jnp.exp(
        jnp.arange(half_width, dtype=jnp.float32) * (-math.log(ROTARY_BASE) / half_width)
    )
    angles = positions.astype(jnp.float32)[:, None] * frequency[None, :]
    cosine, sine = jnp.cos(angles), jnp.sin(angles)
    dma = pltpu.SemaphoreType.DMA
    return pl.pallas_call(
        functools.partial(gather_kernel, heads),
        out_shape=(
            jax.ShapeDtypeStruct((tokens, heads * width), jnp.bfloat16),
            jax.ShapeDtypeStruct((heads * width, basis.shape[1]), jnp.float32),
        ),
        in_specs=[pl.BlockSpec(memory_space=pltpu.VMEM)] * 5,
        out_specs=(pl.BlockSpec(memory_space=pltpu.VMEM),) * 2,
        scratch_shapes=[
            pltpu.VMEM((local, width), jnp.float32),
            pltpu.VMEM((local, LANES), jnp.float32),
            dma((2, 2)),
            dma((2, heads, 2)),
            dma((2, heads, 2)),
            dma((2, heads, 2)),
            dma((2, heads, 2)),
            dma((2, heads, 2)),
            dma((2, heads, 4, 2)),
        ],
        compiler_params=pltpu.CompilerParams(
            collective_id=0, has_side_effects=True, vmem_limit_bytes=24 * 2**20
        ),
    )(
        partial,
        squares,
        jnp.concatenate([cosine, cosine], axis=1),
        jnp.concatenate([-sine, sine], axis=1),
        basis,
    )


def body(hidden, gain, key_weight, value_weight, positions, initial_basis):
    hidden_rows = hidden[0]
    local_tokens = positions.shape[1]
    seqs, batches, heads = lax.axis_size("seq"), lax.axis_size("batch"), lax.axis_size("head")
    tokens = local_tokens * seqs * batches
    if seqs == 2 and batches == 4 and tokens <= initial_basis.shape[0] * heads:
        partial, squares = project(hidden_rows, gain, key_weight, value_weight)
        return iterate(*gather(partial, squares, positions[0], initial_basis, heads, tokens))
    widened = hidden_rows.astype(jnp.float32)
    scaled = (widened * gain).astype(jnp.bfloat16)
    local_squares = jnp.sum(widened * widened, axis=1)
    key_columns = key_weight.shape[1]
    weights = jnp.concatenate([key_weight, value_weight], axis=1)
    own_squares = total_squares(local_squares, local_tokens)
    projected = lax.psum_scatter(
        jnp.dot(scaled, weights, preferred_element_type=jnp.float32),
        "seq",
        scatter_dimension=0,
        tiled=True,
    )
    inverse_scale = lax.rsqrt(own_squares / D + EPSILON)
    projected = projected * inverse_scale[:, None]
    key_rows = rotary(projected[:, :key_columns].reshape(local_tokens, -1, HEAD_DIM), positions[0])
    value_rows = projected[:, key_columns:].reshape(local_tokens, -1, HEAD_DIM)
    joint_rows = (
        jnp.stack([key_rows, value_rows], axis=2).reshape(local_tokens, -1).astype(jnp.bfloat16)
    )
    partial_value = lax.dot_general(
        joint_rows,
        lax.all_gather(joint_rows, "head", axis=1, tiled=True),
        (((0,), (0,)), ((), ())),
        preferred_element_type=jnp.float32,
    )
    token_total = local_tokens * lax.axis_size("seq") * lax.axis_size("batch")
    basis_block = initial_basis
    covariance = lax.psum(partial_value, ("seq", "batch")) / token_total
    for iteration in range(ITERS):
        whole_basis = whole_of(basis_block)
        images = jnp.dot(
            covariance,
            whole_basis,
            precision=lax.Precision.HIGHEST,
            preferred_element_type=jnp.float32,
        )
        gram_matrix = lax.psum(gram_of(images), "head") / whole_basis.shape[0]
        basis_block = orthonormal(images, gram_matrix)
    return basis_block


def solution(mesh):
    return jax.shard_map(
        body,
        mesh=mesh,
        in_specs=(
            P("batch", None, "seq"),
            P("seq"),
            P("seq", "head"),
            P("seq", "head"),
            P("batch", "seq"),
            P("head", None),
        ),
        out_specs=P("head", None),
        check_vma=False,
    )
```

```python
import functools
import math

import jax
import jax.numpy as jnp
from jax import lax
from jax.experimental import pallas as pl
from jax.experimental.pallas import tpu as pltpu
from jax.sharding import PartitionSpec as P

D = 16384
HEAD_DIM = 128
ITERS = 4


EPSILON = 1e-05
ROTARY_BASE = 500000.0


def rotary(head_rows, position_row):
    half_width = head_rows.shape[-1] // 2
    index_row = jnp.arange(half_width, dtype=jnp.float32)
    frequency = jnp.exp(index_row * (-math.log(ROTARY_BASE) / half_width))
    angles = position_row.astype(jnp.float32)[:, None] * frequency[None, :]
    cosine = jnp.cos(angles)[:, None, :]
    sine_part = jnp.sin(angles)[:, None, :]
    first_half = head_rows[..., :half_width]
    second_half = head_rows[..., half_width:]
    return jnp.concatenate(
        [
            first_half * cosine - second_half * sine_part,
            second_half * cosine + first_half * sine_part,
        ],
        axis=-1,
    )


def whole_of(basis_block):
    return lax.all_gather(basis_block, "head", axis=0, tiled=True)


def total_squares(local_squares, local_tokens):
    all_squares = lax.psum(local_squares, "seq")
    return lax.dynamic_slice_in_dim(all_squares, lax.axis_index("seq") * local_tokens, local_tokens)


def gram_of(images):
    return lax.dot_general(
        images,
        images,
        (((0,), (0,)), ((), ())),
        precision=lax.Precision.HIGHEST,
        preferred_element_type=jnp.float32,
    )


def orthonormal(images, gram_matrix):
    factor = jnp.linalg.cholesky(gram_matrix)
    return lax.linalg.triangular_solve(
        factor, images, left_side=False, lower=True, transpose_a=True
    )


LANES = 128
SUBLANES = 8


def dot_of(left, right, left_axis, right_axis, precision=None):
    return lax.dot_general(
        left,
        right,
        (((left_axis,), (right_axis,)), ((), ())),
        precision=precision,
        preferred_element_type=jnp.float32,
    )


def exact(left, right, left_axis, right_axis):
    return dot_of(left, right, left_axis, right_axis, lax.Precision.HIGHEST)


def halves_of(value):
    high = value.astype(jnp.bfloat16)
    return high, (value - high.astype(jnp.float32)).astype(jnp.bfloat16)


def thrice(left, right, left_axis, right_axis):
    left_high, left_low = halves_of(left)
    right_high, right_low = halves_of(right)
    return (
        dot_of(left_high, right_high, left_axis, right_axis)
        + dot_of(left_high, right_low, left_axis, right_axis)
        + dot_of(left_low, right_high, left_axis, right_axis)
    )


def small_inverse(block):
    size = len(block)
    block = [list(line) for line in block]
    extra = [[None] * size for _ in range(size)]
    result = [[None] * size for _ in range(size)]

    def plus(left, right):
        return right if left is None else left if right is None else left + right

    def times(scale, value):
        return None if value is None else scale if isinstance(value, float) else scale * value

    def minus(left, right):
        return left if right is None else -right if left is None else left - right

    for i in range(size):
        extra[i][i] = 1.0
    for k in range(0, size, 2):
        first, cross, last = block[k][k], block[k + 1][k], block[k + 1][k + 1]
        scale = 1.0 / (first * last - cross * cross)
        for i in range(k + 2, size):
            one, two = block[i][k], block[i][k + 1]
            top = (one * last - two * cross) * scale
            low = (two * first - one * cross) * scale
            for j in range(k + 2, i + 1):
                block[i][j] = block[i][j] - (top * block[j][k] + low * block[j][k + 1])
            for j in range(k + 2):
                change = plus(times(top, extra[k][j]), times(low, extra[k + 1][j]))
                extra[i][j] = minus(extra[i][j], change)
        ratio = cross / first
        top_scale, low_scale = lax.rsqrt(first), lax.rsqrt(last - ratio * cross)
        for j in range(k + 2):
            result[k][j] = times(top_scale, extra[k][j])
            result[k + 1][j] = times(low_scale, minus(extra[k + 1][j], times(ratio, extra[k][j])))
    return result


def inverse_factor(matrix):
    size = matrix.shape[0]
    rows = lax.broadcasted_iota(jnp.int32, (SUBLANES, size), 0)
    lanes = lax.broadcasted_iota(jnp.int32, (SUBLANES, size), 1)
    groups = size // SUBLANES
    left = [matrix[SUBLANES * g : SUBLANES * (g + 1)] for g in range(groups)]
    right = [jnp.where(lanes == rows + SUBLANES * g, 1.0, 0.0) for g in range(groups)]

    def spread_row(value, at):
        return jnp.broadcast_to(value[at : at + 1, :], (SUBLANES, size))

    def spread_lane(value, at):
        return jnp.broadcast_to(value[:, at : at + 1], (SUBLANES, size))

    def stacked(values):
        total = jnp.zeros((SUBLANES, size), jnp.float32)
        for i, value in enumerate(values):
            if value is not None:
                total = jnp.where(rows == i, value, total)
        return total

    def combined(columns, value):
        terms = [columns[j] * spread_row(value, j) for j in range(SUBLANES)]
        while len(terms) > 1:
            terms = [terms[i] + terms[i + 1] for i in range(0, len(terms), 2)]
        return terms[0]

    for own in range(groups):
        pivot = own * SUBLANES
        tops = [spread_row(left[own], i) for i in range(SUBLANES)]
        block = [[spread_lane(tops[i], pivot + j) for j in range(i + 1)] for i in range(SUBLANES)]
        small = small_inverse(block)
        down = [stacked([small[i][j] for i in range(SUBLANES)]) for j in range(SUBLANES)]
        across = [stacked([small[j][i] for i in range(SUBLANES)]) for j in range(SUBLANES)]
        scaled_left, scaled_right = combined(down, left[own]), combined(down, right[own])
        right[own] = scaled_right
        if own + 1 == groups:
            break
        mixed_left, mixed_right = combined(across, scaled_left), combined(across, scaled_right)
        mixes = [
            (spread_row(mixed_left, j), spread_row(mixed_right, j)) for j in range(SUBLANES)
        ]
        for g in range(own + 1, groups):
            columns = [spread_lane(left[g], pivot + j) for j in range(SUBLANES)]
            for j in range(SUBLANES):
                left[g] = left[g] - columns[j] * mixes[j][0]
                right[g] = right[g] - columns[j] * mixes[j][1]
    return jnp.concatenate(right, axis=0)


def iterate_kernel(
    joint_ref, basis_ref, out_ref, high_ref, low_ref, rows_ref, gram_ref
):
    tokens, joint = joint_ref.shape
    rank = basis_ref.shape[1]
    panels = rank // LANES
    strip = 256
    for start in range(0, tokens, strip):
        kernel_rows = dot_of(joint_ref[start : start + strip, :], joint_ref[...], 1, 1) * (1.0 / tokens)
        high, low = halves_of(kernel_rows)
        high_ref[start : start + strip, :] = high
        low_ref[start : start + strip, :] = low
    basis_high, basis_low = halves_of(basis_ref[...])
    rows_ref[...] = dot_of(joint_ref[...], basis_high, 1, 0) + dot_of(joint_ref[...], basis_low, 1, 0)

    def step(iteration, carry):
        rows_high, rows_low = halves_of(rows_ref[...])
        images = (
            dot_of(high_ref[...], rows_high, 1, 0)
            + dot_of(high_ref[...], rows_low, 1, 0)
            + dot_of(low_ref[...], rows_high, 1, 0)
        )
        images_high, images_low = halves_of(images)
        gram_ref[...] = (
            dot_of(rows_high, images_high, 0, 0)
            + dot_of(rows_high, images_low, 0, 0)
            + dot_of(rows_low, images_high, 0, 0)
        ) * (1.0 / (tokens * joint))

        @pl.when(iteration < ITERS - 1)
        def _():
            rows_ref[...] = images

        for panel in range(panels):
            start, end = panel * LANES, (panel + 1) * LANES
            inverse = inverse_factor(gram_ref[start:end, start:end])
            columns = thrice(rows_ref[:, start:end], inverse, 1, 1)
            rows_ref[:, start:end] = columns
            if end < rank:
                scaled = exact(inverse, gram_ref[start:end, end:], 1, 0)
                gram_ref[end:, end:] -= exact(scaled, scaled, 0, 0)
                rows_ref[:, end:] -= thrice(columns, scaled, 1, 0)
        return carry

    lax.fori_loop(0, ITERS, step, 0)
    rows_high, rows_low = halves_of(rows_ref[...])
    width = out_ref.shape[0]
    own = joint_ref[:, pl.ds(pl.multiple_of(lax.axis_index("head") * width, width), width)]
    out_ref[...] = (dot_of(own, rows_high, 0, 0) + dot_of(own, rows_low, 0, 0)) * (1.0 / tokens)


def iterate(joint_all, basis_all):
    tokens, joint = joint_all.shape
    rank = basis_all.shape[1]
    return pl.pallas_call(
        iterate_kernel,
        out_shape=jax.ShapeDtypeStruct((joint // lax.axis_size("head"), rank), jnp.float32),
        in_specs=[pl.BlockSpec(memory_space=pltpu.VMEM)] * 2,
        out_specs=pl.BlockSpec(memory_space=pltpu.VMEM),
        scratch_shapes=[
            pltpu.VMEM((tokens, tokens), jnp.bfloat16),
            pltpu.VMEM((tokens, tokens), jnp.bfloat16),
            pltpu.VMEM((tokens, rank), jnp.float32),
            pltpu.VMEM((rank, rank), jnp.float32),
        ],
        compiler_params=pltpu.CompilerParams(vmem_limit_bytes=40 * 2**20),
    )(joint_all, basis_all)


def project_kernel(hidden_ref, gain_ref, key_ref, value_ref, partial_ref, squares_ref):
    key_columns = key_ref.shape[1]

    @pl.when(pl.program_id(0) == 0)
    def _():
        partial_ref[...] = jnp.zeros_like(partial_ref)
        squares_ref[...] = jnp.zeros_like(squares_ref)

    widened = hidden_ref[...].astype(jnp.float32)
    scaled = (widened * gain_ref[...]).astype(jnp.bfloat16)
    partial_ref[:, :key_columns] += dot_of(scaled, key_ref[...], 1, 0)
    partial_ref[:, key_columns:] += dot_of(scaled, value_ref[...], 1, 0)
    squared = widened * widened
    total = squares_ref[...]
    for start in range(0, squared.shape[1], LANES):
        total = total + squared[:, start : start + LANES]
    squares_ref[...] = total


def project(hidden_rows, gain, key_weight, value_weight):
    tokens, depth = hidden_rows.shape
    key_columns, value_columns = key_weight.shape[1], value_weight.shape[1]
    chunk = math.gcd(depth, 1024)
    return pl.pallas_call(
        project_kernel,
        grid=(depth // chunk,),
        out_shape=(
            jax.ShapeDtypeStruct((tokens, key_columns + value_columns), jnp.float32),
            jax.ShapeDtypeStruct((tokens, LANES), jnp.float32),
        ),
        in_specs=[
            pl.BlockSpec((tokens, chunk), lambda step: (0, step)),
            pl.BlockSpec((1, chunk), lambda step: (0, step)),
            pl.BlockSpec((chunk, key_columns), lambda step: (step, 0)),
            pl.BlockSpec((chunk, value_columns), lambda step: (step, 0)),
        ],
        out_specs=(
            pl.BlockSpec((tokens, key_columns + value_columns), lambda step: (0, 0)),
            pl.BlockSpec((tokens, LANES), lambda step: (0, 0)),
        ),
        compiler_params=pltpu.CompilerParams(
            dimension_semantics=("arbitrary",), vmem_limit_bytes=60 * 2**20
        ),
    )(hidden_rows, gain[None, :], key_weight, value_weight)


def gather_kernel(
    heads,
    partial_ref,
    squares_ref,
    cosine_ref,
    sine_ref,
    basis_ref,
    out_ref,
    whole_ref,
    peer_partial,
    peer_squares,
    swap_sems,
    z_sems,
    x_sems,
    y_sems,
    x_half_sems,
    y_half_sems,
    core_sems,
):
    x, b, z = lax.axis_index("seq"), lax.axis_index("batch"), lax.axis_index("head")
    local, width = peer_partial.shape
    half = width // 2
    rank = basis_ref.shape[1]
    piece = width // 8
    other_x, other_y = 1 - x, (b + 2) % 4
    partner = b + 1 - 2 * (b % 2)
    x_peer, y_peer, core_peer = (other_x, b, z), (x, other_y, z), (x, partner, z)

    def z_peer(d):
        return (x, b, (z + d) % heads)

    barrier = pltpu.get_barrier_semaphore()
    peers = [x_peer, y_peer, core_peer] + [z_peer(d) for d in range(1, heads)]
    for peer in peers:
        pl.semaphore_signal(barrier, inc=1, device_id=peer, device_id_type=pl.DeviceIdType.MESH)
    pl.semaphore_wait(barrier, len(peers))

    def copy(source, target, sems, peer):
        return pltpu.make_async_remote_copy(
            src_ref=source,
            dst_ref=target,
            send_sem=sems.at[0],
            recv_sem=sems.at[1],
            device_id=peer,
            device_id_type=pl.DeviceIdType.MESH,
        )

    def region(xs, bs, zs, start=0, size=width):
        row = pl.multiple_of((xs * 4 + bs) * local, local)
        column = pl.multiple_of(zs * width + start, half)
        return out_ref.at[pl.ds(row, local), pl.ds(column, size)]

    def piece_of(xs, bs, zs, start=0, size=rank):
        row = pl.multiple_of(zs * width + (xs * 4 + bs) * piece, piece)
        return whole_ref.at[pl.ds(row, piece), pl.ds(start, size)]

    started = []

    def send(area, sems, peer):
        going = copy(area, area, sems, peer)
        going.start()
        started.append(going)

    def arrive(area, sems, peer):
        copy(area, area, sems, peer).wait_recv()

    def source(d):
        return (z + heads - d) % heads

    order = [0] + sorted(range(1, heads), key=lambda d: (min(d, heads - d), d))
    own_piece = basis_ref.at[pl.ds(pl.multiple_of((x * 4 + b) * piece, piece), piece), :]
    for d in range(1, heads):
        going = copy(own_piece, piece_of(x, b, z), z_sems.at[1, d], z_peer(d))
        going.start()
        started.append(going)

    away = pl.ds(pl.multiple_of(other_x * local, local), local)
    mine = pl.ds(pl.multiple_of(x * local, local), local)
    swaps = [
        copy(partial_ref.at[away, :], peer_partial, swap_sems.at[0], x_peer),
        copy(squares_ref.at[away, :], peer_squares, swap_sems.at[1], x_peer),
    ]
    for swap in swaps:
        swap.start()
    whole_ref[pl.ds(pl.multiple_of(z * width, width), width), :] = basis_ref[...]
    for swap in swaps:
        swap.wait()
    squares = jnp.sum(squares_ref[mine, :] + peer_squares[...], axis=1, keepdims=True)
    projected = (partial_ref[mine, :] + peer_partial[...]) * lax.rsqrt(squares / D + EPSILON)
    row = pl.multiple_of((x * 4 + b) * local, local)
    for g in range(half // HEAD_DIM):
        key = projected[:, g * HEAD_DIM : (g + 1) * HEAD_DIM]
        turned = key * cosine_ref[...] + pltpu.roll(key, HEAD_DIM // 2, 1) * sine_ref[...]
        value = projected[:, half + g * HEAD_DIM : half + (g + 1) * HEAD_DIM]
        column = pl.multiple_of(z * width + 2 * g * HEAD_DIM, HEAD_DIM)
        out_ref[pl.ds(row, local), pl.ds(column, HEAD_DIM)] = turned.astype(jnp.bfloat16)
        column = pl.multiple_of(z * width + (2 * g + 1) * HEAD_DIM, HEAD_DIM)
        out_ref[pl.ds(row, local), pl.ds(column, HEAD_DIM)] = value.astype(jnp.bfloat16)

    for d in range(1, heads):
        send(region(x, b, z), z_sems.at[0, d], z_peer(d))

    def spread(kind, area, middle, d):
        mine = area(x, b, source(d))
        if d:
            arrive(mine, z_sems.at[kind, d], z_peer(d))
        send(mine, x_sems.at[kind, d], x_peer)
        send(mine, y_sems.at[kind, d], y_peer)
        send(mine, core_sems.at[kind, d, 0], core_peer)

    def relay(kind, area, middle, d):
        s = source(d)
        arrive(area(other_x, b, s), x_sems.at[kind, d], x_peer)
        send(area(other_x, b, s, middle, middle), y_half_sems.at[kind, d], y_peer)
        send(area(other_x, b, s), core_sems.at[kind, d, 1], core_peer)
        arrive(area(x, other_y, s), y_sems.at[kind, d], y_peer)
        send(area(x, other_y, s, 0, middle), x_half_sems.at[kind, d], x_peer)
        send(area(x, other_y, s), core_sems.at[kind, d, 2], core_peer)

    def finish(kind, area, middle, d):
        s = source(d)
        arrive(area(other_x, other_y, s, 0, middle), x_half_sems.at[kind, d], x_peer)
        arrive(area(other_x, other_y, s, middle, middle), y_half_sems.at[kind, d], y_peer)
        send(area(other_x, other_y, s), core_sems.at[kind, d, 3], core_peer)

    joint, pieces = (0, region, half), (1, piece_of, rank // 2)
    items = [joint + (0,)] + [pieces + (d,) for d in order[1:]] + [joint + (d,) for d in order[1:]]
    for turn in range(len(items) + 2):
        if turn < len(items):
            spread(*items[turn])
        if 1 <= turn < len(items) + 1:
            relay(*items[turn - 1])
        if turn >= 2:
            finish(*items[turn - 2])
    far = (partner + 2) % 4
    for kind, area, middle, d in items:
        s = source(d)
        places = [(x, partner), (other_x, partner), (x, far), (other_x, far)]
        for place, (xs, bs) in enumerate(places):
            arrive(area(xs, bs, s), core_sems.at[kind, d, place], core_peer)
    for going in started:
        going.wait_send()


def gather(partial, squares, positions, basis, heads, tokens):
    local, width = positions.shape[0], partial.shape[1]
    half_width = HEAD_DIM // 2
    frequency = jnp.exp(
        jnp.arange(half_width, dtype=jnp.float32) * (-math.log(ROTARY_BASE) / half_width)
    )
    angles = positions.astype(jnp.float32)[:, None] * frequency[None, :]
    cosine, sine = jnp.cos(angles), jnp.sin(angles)
    dma = pltpu.SemaphoreType.DMA
    return pl.pallas_call(
        functools.partial(gather_kernel, heads),
        out_shape=(
            jax.ShapeDtypeStruct((tokens, heads * width), jnp.bfloat16),
            jax.ShapeDtypeStruct((heads * width, basis.shape[1]), jnp.float32),
        ),
        in_specs=[pl.BlockSpec(memory_space=pltpu.VMEM)] * 5,
        out_specs=(pl.BlockSpec(memory_space=pltpu.VMEM),) * 2,
        scratch_shapes=[
            pltpu.VMEM((local, width), jnp.float32),
            pltpu.VMEM((local, LANES), jnp.float32),
            dma((2, 2)),
            dma((2, heads, 2)),
            dma((2, heads, 2)),
            dma((2, heads, 2)),
            dma((2, heads, 2)),
            dma((2, heads, 2)),
            dma((2, heads, 4, 2)),
        ],
        compiler_params=pltpu.CompilerParams(
            collective_id=0, has_side_effects=True, vmem_limit_bytes=24 * 2**20
        ),
    )(
        partial,
        squares,
        jnp.concatenate([cosine, cosine], axis=1),
        jnp.concatenate([-sine, sine], axis=1),
        basis,
    )


def body(hidden, gain, key_weight, value_weight, positions, initial_basis):
    hidden_rows = hidden[0]
    local_tokens = positions.shape[1]
    seqs, batches, heads = lax.axis_size("seq"), lax.axis_size("batch"), lax.axis_size("head")
    tokens = local_tokens * seqs * batches
    if seqs == 2 and batches == 4 and tokens <= initial_basis.shape[0] * heads:
        partial, squares = project(hidden_rows, gain, key_weight, value_weight)
        return iterate(*gather(partial, squares, positions[0], initial_basis, heads, tokens))
    widened = hidden_rows.astype(jnp.float32)
    scaled = (widened * gain).astype(jnp.bfloat16)
    local_squares = jnp.sum(widened * widened, axis=1)
    key_columns = key_weight.shape[1]
    weights = jnp.concatenate([key_weight, value_weight], axis=1)
    own_squares = total_squares(local_squares, local_tokens)
    projected = lax.psum_scatter(
        jnp.dot(scaled, weights, preferred_element_type=jnp.float32),
        "seq",
        scatter_dimension=0,
        tiled=True,
    )
    inverse_scale = lax.rsqrt(own_squares / D + EPSILON)
    projected = projected * inverse_scale[:, None]
    key_rows = rotary(projected[:, :key_columns].reshape(local_tokens, -1, HEAD_DIM), positions[0])
    value_rows = projected[:, key_columns:].reshape(local_tokens, -1, HEAD_DIM)
    joint_rows = (
        jnp.stack([key_rows, value_rows], axis=2).reshape(local_tokens, -1).astype(jnp.bfloat16)
    )
    partial_value = lax.dot_general(
        joint_rows,
        lax.all_gather(joint_rows, "head", axis=1, tiled=True),
        (((0,), (0,)), ((), ())),
        preferred_element_type=jnp.float32,
    )
    token_total = local_tokens * lax.axis_size("seq") * lax.axis_size("batch")
    basis_block = initial_basis
    covariance = lax.psum(partial_value, ("seq", "batch")) / token_total
    for iteration in range(ITERS):
        whole_basis = whole_of(basis_block)
        images = jnp.dot(
            covariance,
            whole_basis,
            precision=lax.Precision.HIGHEST,
            preferred_element_type=jnp.float32,
        )
        gram_matrix = lax.psum(gram_of(images), "head") / whole_basis.shape[0]
        basis_block = orthonormal(images, gram_matrix)
    return basis_block


def solution(mesh):
    return jax.shard_map(
        body,
        mesh=mesh,
        in_specs=(
            P("batch", None, "seq"),
            P("seq"),
            P("seq", "head"),
            P("seq", "head"),
            P("batch", "seq"),
            P("head", None),
        ),
        out_specs=P("head", None),
        check_vma=False,
    )
```
